256 devices in a mesh: dp: 16 (over y, x), vocab: 16 (over z, core).
Axes of the slice: x: 4, y: 4, z: 8, core: 2. Of those that a mesh axis runs over, the one named last changes fastest.
Arguments:
- hidden: bfloat16 [256, 128, 4096], P('vocab', None, 'dp'), may hold values from -6 to 6
- weights: bfloat16 [65536, 4096], P('vocab', 'dp'), may hold values from -0.09375 to 0.09375
- bias: float32 [65536], P('vocab'), may hold values from -4 to 4
- first_moment: bfloat16 [65536, 4096], P('vocab', 'dp'), may hold values from -6 to 6
- second_moment: bfloat16 [65536, 4096], P('vocab', 'dp'), may hold values from 0.049804688 to 2
- rep_cot: bfloat16 [256, 16, 512], P(None, 'vocab'), may hold values from -768 to 768
- active_blocks: int32 [256, 16, 4], P(None, 'vocab'), may hold values from 0 to 31, as said below
- block_counts: int32 [256, 16], replicated, may hold values from 0 to 4, as said below
- passage_len: int32 [256], replicated, may hold values from 16 to 128, as said below
Outputs:
- reps: float32 [16, 16, 4, 512], P('dp', 'vocab')
- grad_hidden: bfloat16 [256, 128, 4096], P('vocab', None, 'dp')
- new_first: bfloat16 [65536, 4096], P('vocab', 'dp')
- new_second: bfloat16 [65536, 4096], P('vocab', 'dp')
The draws below stay inside these ranges and needn't reach their ends.
Inputs may be any that keep to these rules, and one draw needn't show every extreme that they name: `block_counts`: within each batch of 16 passages, every owner has between max(1, 2) and 4 live passages, and in every batch some owner has exactly 4; some passage at each owner of each batch has count 4. `active_blocks`: the 4 block numbers of one passage at one owner are distinct. `passage_len`: every batch has a passage of length 128.
All inputs are finite; a program needn't handle non-finite values.
Results may differ from the reference program's by a relative error of at most 0.012.
Values may be sent and summed in bfloat16 or wider, within the bound.
No kernel may reach another device: no remote copies, remote signals or barrier semaphores. Data moves between devices by JAX's collectives and lax.ppermute only.
A program may use at most 128 MiB of HBM per device.

```python
import math
import jax
import jax.numpy as jnp
from jax import lax

D = 4096
BLOCK = 128
OWN_BLOCKS = 32
SLOT_BLOCKS = 4
OWN_SLOTS = 4
PLEN = 128
PAS_B = 16
PASSAGES = 256
VOCAB = 65536
N_DP = 16
N_VOCAB = 16


def draw_block_counts(key, part):
    base_key = jax.random.fold_in(key, 11)
    key_live, key_hot, key_perm, key_amount = jax.random.split(base_key, 4)
    batches = PASSAGES // PAS_B
    least_live = max(1, OWN_SLOTS // 2)
    live_total = jax.random.randint(key_live, (batches, N_VOCAB), least_live, OWN_SLOTS + 1, dtype=jnp.int32)
    hot_owner = jax.random.randint(key_hot, (batches,), 0, N_VOCAB, dtype=jnp.int32)
    owner_line = jnp.arange(N_VOCAB, dtype=jnp.int32)
    live_total = jnp.where(owner_line[None, :] == hot_owner[:, None], OWN_SLOTS, live_total)
    perm_keys = jax.random.split(key_perm, batches * N_VOCAB)
    orders = jax.vmap(lambda sub_key: jax.random.permutation(sub_key, PAS_B))(perm_keys)
    orders = orders.reshape(batches, N_VOCAB, PAS_B).astype(jnp.int32)
    position = jnp.argsort(orders, axis=-1).astype(jnp.int32)
    live_mask = position < live_total[:, :, None]
    amount = jax.random.randint(key_amount, (batches, N_VOCAB, PAS_B), 1, SLOT_BLOCKS + 1, dtype=jnp.int32)
    amount = jnp.where(position == 0, SLOT_BLOCKS, amount)
    counts = jnp.where(live_mask, amount, 0)
    return jnp.transpose(counts, (0, 2, 1)).reshape(PASSAGES, N_VOCAB).astype(jnp.int32)


def draw_active_blocks(key, part):
    base_key = jax.random.fold_in(key, 23)
    perm_keys = jax.random.split(base_key, PASSAGES * N_VOCAB)
    picked = jax.vmap(lambda sub_key: jax.random.permutation(sub_key, OWN_BLOCKS)[:SLOT_BLOCKS])(perm_keys)
    return picked.reshape(PASSAGES, N_VOCAB, SLOT_BLOCKS).astype(jnp.int32)


def draw_passage_len(key, part):
    base_key = jax.random.fold_in(key, 37)
    key_len, key_long = jax.random.split(base_key, 2)
    batches = PASSAGES // PAS_B
    shortest = max(1, PLEN // 8)
    lengths = jax.random.randint(key_len, (batches, PAS_B), shortest, PLEN + 1, dtype=jnp.int32)
    longest = jax.random.randint(key_long, (batches,), 0, PAS_B, dtype=jnp.int32)
    place_line = jnp.arange(PAS_B, dtype=jnp.int32)
    lengths = jnp.where(place_line[None, :] == longest[:, None], PLEN, lengths)
    return lengths.reshape(PASSAGES).astype(jnp.int32)


def levels(key, extent, shards, low, largest):
    gain = 1.0
    for axis_at, parts in shards:
        heights = jax.random.uniform(jax.random.fold_in(jax.random.fold_in(key, 6), axis_at), (parts,), jnp.float32, low / len(shards), largest / len(shards))
        gain = gain * jnp.repeat(jnp.exp(heights), extent[axis_at] // parts).reshape((-1,) + (1,) * (len(extent) - 1 - axis_at))
    return gain


def scatter_about(rng, extent, deviation, bound, cuts=(), held_as=jnp.bfloat16):
    level = levels(rng, extent, cuts, -0.22, 0.18) if cuts else 1.0
    entries = jax.random.normal(rng, extent, jnp.float32) * deviation * level
    return jnp.minimum(jnp.maximum(entries, -bound), bound).astype(held_as)


def setup_inputs(seed: int = 0) -> dict:
    key_of = jax.random.split(jax.random.key(seed), 10)
    hidden = scatter_about(key_of[0], (PASSAGES, PLEN, D), 1.0, 6.0, ((0, 16), (2, 16)))
    weights = scatter_about(key_of[1], (VOCAB, D), D ** -0.5, 0.09375, ((0, 16), (1, 16)))
    bias = scatter_about(key_of[2], (VOCAB,), 1.0, 4.0, ((0, 16),), jnp.float32)
    first_moment = scatter_about(key_of[3], (VOCAB, D), 1.0, 6.0, ((0, 16), (1, 16)))
    second_moment = jnp.clip(jnp.exp(math.log(2.0) - 3.6927934 * jax.random.uniform(key_of[4], (VOCAB, D), jnp.float32) ** levels(key_of[4], (VOCAB, D), ((0, 16), (1, 16)), -0.2, 0.2)), 0.049804688, 2.0).astype(jnp.bfloat16)
    rep_cot = scatter_about(key_of[5], (PASSAGES, N_VOCAB, SLOT_BLOCKS * BLOCK), 128.0, 768.0, ((1, 16),))
    active_blocks = draw_active_blocks(jax.random.fold_in(key_of[9], 71), 0)
    block_counts = draw_block_counts(jax.random.fold_in(key_of[9], 71), 0)
    passage_len = draw_passage_len(jax.random.fold_in(key_of[9], 71), 0)
    return {"hidden": hidden, "weights": weights, "bias": bias, "first_moment": first_moment, "second_moment": second_moment, "rep_cot": rep_cot, "active_blocks": active_blocks, "block_counts": block_counts, "passage_len": passage_len}


beta_one = 0.9
beta_two = 0.999


def slot_tables(block_counts, batches, owners, per_batch, slot_total):
    live_mask = (block_counts > 0).astype(jnp.int32).reshape(batches, per_batch, owners)
    slot_rank = (jnp.cumsum(live_mask, axis=1, dtype=jnp.int32) - live_mask).astype(jnp.int32)
    slot_place = jnp.arange(slot_total, dtype=jnp.int32)
    chosen = (live_mask[:, :, :, None] == 1) & (slot_rank[:, :, :, None] == slot_place[None, None, None, :])
    return jnp.transpose(chosen, (0, 2, 3, 1)).astype(jnp.int32)


def slot_info(onehot, ids_col, counts_col, lengths, plen_size, block_size):
    slot_ids = jnp.sum(onehot[:, :, :, None] * ids_col[:, None, :, :], axis=2).astype(jnp.int32)
    slot_count = jnp.sum(onehot * counts_col[:, None, :], axis=2).astype(jnp.int32)
    slot_len = jnp.sum(onehot * lengths[:, None, :], axis=2).astype(jnp.int32)
    filled = jnp.sum(onehot, axis=2).astype(jnp.int32)
    divisor = jnp.where(filled > 0, slot_len, 1).astype(jnp.float32)
    token_ok = jnp.arange(plen_size, dtype=jnp.int32)[None, None, :] < slot_len[:, :, None]
    col_block = jnp.arange(slot_ids.shape[2] * block_size, dtype=jnp.int32) // block_size
    col_ok = col_block[None, None, :] < slot_count[:, :, None]
    return slot_ids, divisor, token_ok, col_ok


def activate(logits, bias_cols, cot, token_ok, col_ok, divisor):
    shifted = logits + bias_cols[:, :, None, :]
    softened = jax.nn.softplus(shifted)
    kept_mask = (token_ok[:, :, :, None] & col_ok[:, :, None, :]).astype(jnp.float32)
    pool_weight = kept_mask / divisor[:, :, None, None]
    pooled = jnp.sum(jnp.log1p(softened) * pool_weight, axis=2)
    slope = (cot[:, :, None, :] * pool_weight * jax.nn.sigmoid(shifted) / (1.0 + softened)).astype(jnp.bfloat16)
    return pooled, slope


def reference(hidden, weights, bias, first_moment, second_moment, rep_cot, active_blocks, block_counts, passage_len):
    owners = N_VOCAB
    per_batch = PAS_B
    col_width = SLOT_BLOCKS * BLOCK
    feature_parts = N_DP
    dslice = D // N_DP
    chosen = slot_tables(block_counts, owners, owners, per_batch, OWN_SLOTS)
    rows_all = hidden.reshape(owners, per_batch, PLEN * D).astype(jnp.float32)
    lengths = passage_len.reshape(owners, per_batch)
    ids_all = active_blocks.reshape(owners, per_batch, owners, SLOT_BLOCKS)
    counts_all = block_counts.reshape(owners, per_batch, owners)
    cot_all = rep_cot.reshape(owners, per_batch, owners, col_width).astype(jnp.float32)
    w_all = weights.reshape(owners, OWN_BLOCKS, BLOCK, D)
    b_all = bias.reshape(owners, OWN_BLOCKS, BLOCK)
    m_all = first_moment.reshape(owners, OWN_BLOCKS * BLOCK, D)
    v_all = second_moment.reshape(owners, OWN_BLOCKS * BLOCK, D)

    def per_owner(grad_sum, inputs_here):
        owner_index, w_own, b_own, m_own, v_own = inputs_here
        onehot = lax.dynamic_index_in_dim(chosen, owner_index, 1, keepdims=False)
        ids_col = lax.dynamic_index_in_dim(ids_all, owner_index, 2, keepdims=False)
        counts_col = lax.dynamic_index_in_dim(counts_all, owner_index, 2, keepdims=False)
        cot_col = lax.dynamic_index_in_dim(cot_all, owner_index, 2, keepdims=False)
        slot_ids, divisor, token_ok, col_ok = slot_info(onehot, ids_col, counts_col, lengths, PLEN, BLOCK)
        select = onehot.astype(jnp.float32)
        slot_rows = jnp.einsum("jsp,jpx->jsx", select, rows_all).reshape(owners, OWN_SLOTS, PLEN, D)
        slot_cot = jnp.einsum("jsp,jpc->jsc", select, cot_col)
        w_sel = w_own[slot_ids].reshape(owners, OWN_SLOTS, col_width, D).astype(jnp.float32)
        bias_cols = b_own[slot_ids].reshape(owners, OWN_SLOTS, col_width)
        partial_value = jnp.einsum("jstid,jscid->ijstc",
                             slot_rows.reshape(owners, OWN_SLOTS, PLEN, feature_parts, dslice),
                             w_sel.reshape(owners, OWN_SLOTS, col_width, feature_parts, dslice))
        rounded = lax.optimization_barrier(partial_value.astype(jnp.bfloat16)).astype(jnp.float32)
        logits = jnp.sum(rounded, axis=0)
        pooled, slope = activate(logits, bias_cols, slot_cot, token_ok, col_ok, divisor)
        slope_f = slope.astype(jnp.float32)
        back_part = jnp.einsum("jstc,jscd->jstd", slope_f, w_sel).astype(jnp.bfloat16)
        grad_sum = grad_sum + jnp.einsum("jsp,jstd->jptd", select, back_part.astype(jnp.float32))
        outer_sum = jnp.einsum("jstd,jstc->jscd", slot_rows, slope_f)
        grad_w = jnp.zeros((OWN_BLOCKS, BLOCK, D), jnp.float32).at[slot_ids.reshape(-1)].add(
            outer_sum.reshape(owners * OWN_SLOTS * SLOT_BLOCKS, BLOCK, D))
        grad_w = grad_w.reshape(OWN_BLOCKS * BLOCK, D)
        first_new = (beta_one * m_own.astype(jnp.float32) + (1.0 - beta_one) * grad_w).astype(jnp.bfloat16)
        second_new = (beta_two * v_own.astype(jnp.float32) + (1.0 - beta_two) * grad_w * grad_w).astype(jnp.bfloat16)
        return grad_sum, (pooled, first_new, second_new)

    start_grad = jnp.zeros((owners, per_batch, PLEN, D), jnp.float32)
    owner_list = jnp.arange(owners, dtype=jnp.int32)
    grad_sum, outputs = lax.scan(per_owner, start_grad, (owner_list, w_all, b_all, m_all, v_all))
    pooled_all, first_all, second_all = outputs
    reps = jnp.transpose(pooled_all, (1, 0, 2, 3))
    grad_hidden = grad_sum.reshape(PASSAGES, PLEN, D).astype(jnp.bfloat16)
    return (reps, grad_hidden, first_all.reshape(VOCAB, D), second_all.reshape(VOCAB, D))
```

```python
import functools

import jax
import jax.numpy as jnp
from jax import lax
from jax.experimental import pallas as pl
from jax.experimental.pallas import tpu as pltpu
from jax.sharding import PartitionSpec as P

BLOCK = 128
OWN_BLOCKS = 32
SLOT_BLOCKS = 4
OWN_SLOTS = 4
TILE = 16
CAP_SHARE = 15
CAP_PARTS = 32

beta_one = 0.9
beta_two = 0.999

PASS, COUNT, ROWS, OFF, LEN, IDS = 0, 1, 2, 3, 4, 5
WIDTH = 16
UNIT, START, TLEN, BIAS_ROW, COT_ROW = 0, 1, 2, 3, 4
TWIDTH = 8

CONTRACT_LAST = (((1,), (1,)), ((), ()))
CONTRACT_FIRST = (((0,), (0,)), ((), ()))


def slot_table(counts_all, ids, lengths, me):
    batches, per_batch, owners = counts_all.shape
    live = (counts_all > 0).astype(jnp.int32)
    place = jnp.arange(per_batch, dtype=jnp.int32)
    earlier = (place[None, :] < place[:, None]).astype(jnp.int32)
    rank = jnp.sum(live[:, None, :, :] * earlier[None, :, :, None], axis=2)
    slot_place = jnp.arange(OWN_SLOTS, dtype=jnp.int32)
    padded = (lengths + TILE - 1) // TILE * TILE
    kept = live * (rank < OWN_SLOTS)
    totals = jnp.sum(kept * counts_all * padded[:, :, None], axis=(0, 1))
    counts = lax.dynamic_index_in_dim(counts_all, me, 2, keepdims=False)
    live_me = lax.dynamic_index_in_dim(live, me, 2, keepdims=False)
    rank_me = lax.dynamic_index_in_dim(rank, me, 2, keepdims=False)
    chosen = (
        (live_me[:, None, :] == 1) & (rank_me[:, None, :] == slot_place[None, :, None])
    ).astype(jnp.int32)
    first = jnp.arange(batches, dtype=jnp.int32)[:, None] * per_batch
    passage = jnp.sum(chosen * place[None, None, :], axis=2) + first
    count = jnp.sum(chosen * counts[:, None, :], axis=2)
    length = jnp.sum(chosen * lengths[:, None, :], axis=2)
    rows = jnp.sum(chosen * padded[:, None, :], axis=2)
    slot_ids = jnp.sum(chosen[:, :, :, None] * ids[:, None, :, :], axis=2)
    slots = batches * OWN_SLOTS
    need = (count * rows).reshape(slots)
    order = jnp.arange(slots, dtype=jnp.int32)
    off = jnp.sum(jnp.where(order[None, :] < order[:, None], need[None, :], 0), axis=1)
    columns = [
        passage.reshape(slots, 1),
        count.reshape(slots, 1),
        rows.reshape(slots, 1),
        off.reshape(slots, 1),
        length.reshape(slots, 1),
        slot_ids.reshape(slots, SLOT_BLOCKS),
        jnp.zeros((slots, WIDTH - IDS - SLOT_BLOCKS), jnp.int32),
    ]
    return jnp.concatenate(columns, axis=1), jnp.max(totals)


def tile_table(slots, first_tile, tiles):
    at = first_tile + jnp.arange(tiles, dtype=jnp.int32)
    starts = slots[:, OFF] // TILE
    holder = jnp.sum((starts[None, :] <= at[:, None]).astype(jnp.int32), axis=1) - 1
    order = jnp.arange(slots.shape[0], dtype=jnp.int32)
    pick = (holder[:, None] == order[None, :]).astype(jnp.int32)
    mine = jnp.sum(pick[:, :, None] * slots[None, :, :], axis=1)
    height = mine[:, ROWS] // TILE
    rel = at - mine[:, OFF] // TILE
    q = sum((rel >= height * n).astype(jnp.int32) for n in range(1, SLOT_BLOCKS))
    start = (rel - q * height) * TILE
    length = jnp.where(rel < height * mine[:, COUNT], mine[:, LEN], 0)
    which = jnp.arange(SLOT_BLOCKS, dtype=jnp.int32)
    block = jnp.sum(
        jnp.where(which[None, :] == q[:, None], mine[:, IDS : IDS + SLOT_BLOCKS], 0), axis=1
    )
    columns = [
        holder * SLOT_BLOCKS + q,
        start,
        length,
        block,
        mine[:, PASS] * SLOT_BLOCKS + q,
    ]
    filler = jnp.zeros((tiles,), jnp.int32)
    return jnp.stack(columns + [filler] * (TWIDTH - len(columns)), axis=1).reshape(-1)


def pair_weights(w_ref, tab_ref, base, pair):
    one = tab_ref[base + IDS + 2 * pair]
    two = tab_ref[base + IDS + 2 * pair + 1]
    return jnp.concatenate([w_ref[one], w_ref[two]], axis=0)


def pair_slopes(buf, tab_ref, base, pair):
    plen = BLOCK
    count, rows = tab_ref[base + COUNT], tab_ref[base + ROWS]
    off, length = tab_ref[base + OFF], tab_ref[base + LEN]
    token = lax.broadcasted_iota(jnp.int32, (plen, BLOCK), 0)
    halves = []
    for q in (2 * pair, 2 * pair + 1):
        at = pl.multiple_of(off + q * rows, TILE)
        value = buf[pl.ds(at, plen), :]
        bound = jnp.where(q < count, length, 0)
        halves.append(jnp.where(token < bound, value.astype(jnp.float32), 0.0).astype(jnp.bfloat16))
    return jnp.concatenate(halves, axis=1)


def forward_kernel(cap, tab_ref, *refs):
    hidden_refs, w_ref = refs[:OWN_SLOTS], refs[OWN_SLOTS]
    main_ref, rest_ref, buf, sems = refs[OWN_SLOTS + 1 :]
    j = pl.program_id(0)
    for s in range(OWN_SLOTS):
        base = (j * OWN_SLOTS + s) * WIDTH
        count, rows, off = tab_ref[base + COUNT], tab_ref[base + ROWS], tab_ref[base + OFF]
        for pair in range(SLOT_BLOCKS // 2):

            @pl.when(count > 2 * pair)
            def _():
                w2 = pair_weights(w_ref, tab_ref, base, pair)
                value = lax.dot_general(
                    hidden_refs[s][0], w2, CONTRACT_LAST, preferred_element_type=jnp.float32
                ).astype(jnp.bfloat16)
                at = pl.multiple_of(off + 2 * pair * rows, TILE)
                buf[pl.ds(at, BLOCK), :] = value[:, :BLOCK]
                at = pl.multiple_of(off + (2 * pair + 1) * rows, TILE)
                buf[pl.ds(at, BLOCK), :] = value[:, BLOCK:]

    last = pl.num_programs(0) - 1

    @pl.when(j == last)
    def _():
        copy = pltpu.make_async_copy(buf.at[pl.ds(0, cap)], main_ref, sems.at[0])
        copy.start()
        copy.wait()
        base = (last * OWN_SLOTS + OWN_SLOTS - 1) * WIDTH
        total = tab_ref[base + OFF] + tab_ref[base + COUNT] * tab_ref[base + ROWS]

        @pl.when(total > cap)
        def _():
            more = pltpu.make_async_copy(
                buf.at[pl.ds(cap, rest_ref.shape[0])], rest_ref, sems.at[1]
            )
            more.start()
            more.wait()


def activate_kernel(tiles, tile_ref, lg_ref, bias_ref, cot_ref, slope_ref, pooled_ref):
    pooled_ref[...] = jnp.zeros_like(pooled_ref)

    def step(i, carry):
        base = i * TWIDTH
        unit, start = tile_ref[base + UNIT], tile_ref[base + START]
        length, bias_row = tile_ref[base + TLEN], tile_ref[base + BIAS_ROW]
        cot_row = tile_ref[base + COT_ROW]
        at = pl.multiple_of(i * TILE, TILE)
        x = lg_ref[pl.ds(at, TILE), :].astype(jnp.float32) + bias_ref[pl.ds(bias_row, 1), :]
        token = lax.broadcasted_iota(jnp.int32, x.shape, 0) + start
        keep = token < length
        divisor = jnp.full((1, BLOCK), jnp.maximum(length, 1), jnp.int32).astype(jnp.float32)
        weight = 1.0 / divisor
        small = jnp.exp(-jnp.abs(x))
        soft = jnp.maximum(x, 0.0) + jnp.log1p(small)
        sig = jnp.where(x >= 0, 1.0, small) / (1.0 + small)
        gain = jnp.where(keep, jnp.log1p(soft) * weight, 0.0)
        pooled_ref[pl.ds(unit, 1), :] += jnp.sum(gain, axis=0, keepdims=True)
        cot = cot_ref[pl.ds(cot_row, 1), :] * weight
        slope = jnp.where(keep, cot * sig / (1.0 + soft), 0.0)
        slope_ref[pl.ds(at, TILE), :] = slope.astype(jnp.bfloat16)
        return carry

    lax.fori_loop(0, tiles, step, 0, unroll=4)


def load_slopes(cap, tab_ref, main_ref, rest_ref, buf, sems, slots):
    copy = pltpu.make_async_copy(main_ref, buf.at[pl.ds(0, cap)], sems.at[0])
    copy.start()
    copy.wait()
    base = (slots - 1) * WIDTH
    total = tab_ref[base + OFF] + tab_ref[base + COUNT] * tab_ref[base + ROWS]

    @pl.when(total > cap)
    def _():
        more = pltpu.make_async_copy(rest_ref, buf.at[pl.ds(cap, rest_ref.shape[0])], sems.at[1])
        more.start()
        more.wait()


def hidden_grad_kernel(cap, tab_ref, main_ref, rest_ref, w_ref, out_ref, buf, sems):
    j = pl.program_id(0)

    @pl.when(j == 0)
    def _():
        load_slopes(cap, tab_ref, main_ref, rest_ref, buf, sems, pl.num_programs(0) * OWN_SLOTS)

    out_ref[...] = jnp.zeros_like(out_ref)
    per_batch = out_ref.shape[0]
    for s in range(OWN_SLOTS):
        base = (j * OWN_SLOTS + s) * WIDTH
        count = tab_ref[base + COUNT]
        local = tab_ref[base + PASS] - j * per_batch

        @pl.when((count > 0) & (count <= 2))
        def _():
            slopes = pair_slopes(buf, tab_ref, base, 0)
            w2 = pair_weights(w_ref, tab_ref, base, 0)
            value = jnp.dot(slopes, w2, preferred_element_type=jnp.float32)
            out_ref[local] = value.astype(jnp.bfloat16)

        @pl.when(count > 2)
        def _():
            slopes = jnp.concatenate(
                [pair_slopes(buf, tab_ref, base, 0), pair_slopes(buf, tab_ref, base, 1)], axis=1
            )
            w4 = jnp.concatenate(
                [pair_weights(w_ref, tab_ref, base, 0), pair_weights(w_ref, tab_ref, base, 1)],
                axis=0,
            )
            value = jnp.dot(slopes, w4, preferred_element_type=jnp.float32)
            out_ref[local] = value.astype(jnp.bfloat16)


def weight_grad_kernel(cap, batches, tab_ref, *refs):
    hidden_refs = refs[:OWN_SLOTS]
    main_ref, rest_ref, m_ref, v_ref, first_ref, second_ref, buf, acc, sems = refs[OWN_SLOTS:]
    i = pl.program_id(0)

    @pl.when(i == 0)
    def _():
        load_slopes(cap, tab_ref, main_ref, rest_ref, buf, sems, batches * OWN_SLOTS)
        acc[...] = jnp.zeros_like(acc)

    @pl.when(i < batches)
    def _():
        for s in range(OWN_SLOTS):
            base = (i * OWN_SLOTS + s) * WIDTH
            count = tab_ref[base + COUNT]
            for pair in range(SLOT_BLOCKS // 2):

                @pl.when(count > 2 * pair)
                def _():
                    slopes = pair_slopes(buf, tab_ref, base, pair)
                    value = lax.dot_general(
                        slopes,
                        hidden_refs[s][0],
                        CONTRACT_FIRST,
                        preferred_element_type=jnp.float32,
                    )
                    acc[tab_ref[base + IDS + 2 * pair]] += value[:BLOCK]
                    acc[tab_ref[base + IDS + 2 * pair + 1]] += value[BLOCK:]

    @pl.when(i >= batches)
    def _():
        group = m_ref.shape[0]
        at = (i - batches) * group
        grad = acc[pl.ds(at, group)]
        m = m_ref[...].astype(jnp.float32)
        v = v_ref[...].astype(jnp.float32)
        first_ref[...] = (beta_one * m + (1.0 - beta_one) * grad).astype(jnp.bfloat16)
        second_ref[...] = (beta_two * v + (1.0 - beta_two) * grad * grad).astype(jnp.bfloat16)


def shards(
    hidden,
    weights,
    bias,
    first_moment,
    second_moment,
    rep_cot,
    active_blocks,
    block_counts,
    passage_len,
):
    batches = lax.axis_size("vocab")
    parts = lax.axis_size("dp")
    per_batch, plen, dslice = hidden.shape
    col_width = SLOT_BLOCKS * BLOCK
    slots = batches * OWN_SLOTS
    full = slots * SLOT_BLOCKS * plen
    cap = full * CAP_SHARE // CAP_PARTS
    rest = full - cap
    slack = 2 * BLOCK
    me = lax.axis_index("vocab")
    rank = lax.axis_index("dp")

    rows_all = lax.all_gather(hidden, "vocab", axis=0, tiled=True)

    table, most = slot_table(
        block_counts.reshape(batches, per_batch, batches),
        active_blocks.reshape(batches, per_batch, SLOT_BLOCKS),
        passage_len.reshape(batches, per_batch),
        me,
    )
    tab = table.reshape(-1)
    cot_rows = rep_cot.astype(jnp.float32).reshape(-1, BLOCK)
    bias_rows = bias.reshape(OWN_BLOCKS, BLOCK)
    w_blocks = weights.reshape(OWN_BLOCKS, BLOCK, dslice)

    any_spec = pl.BlockSpec(memory_space=pl.ANY)
    vmem = pl.BlockSpec(memory_space=pltpu.VMEM)
    smem = pl.BlockSpec(memory_space=pltpu.SMEM)

    def passage_spec(s):
        def index(i, t):
            row = jnp.minimum(i, batches - 1) * OWN_SLOTS + s
            return (t[row * WIDTH + PASS], 0, 0)

        return pl.BlockSpec((1, plen, dslice), index)

    passage_specs = [passage_spec(s) for s in range(OWN_SLOTS)]
    w_spec = pl.BlockSpec(
        w_blocks.shape, lambda i, t: (0, 0, 0), pipeline_mode=pl.Buffered(buffer_count=1)
    )
    buf_shape = pltpu.VMEM((full + slack, BLOCK), jnp.bfloat16)
    sems = pltpu.SemaphoreType.DMA((2,))
    limit = 60 * 1024 * 1024
    flops = 2 * slots * plen * col_width * dslice

    main, over = pl.pallas_call(
        functools.partial(forward_kernel, cap),
        out_shape=(
            jax.ShapeDtypeStruct((cap, BLOCK), jnp.bfloat16),
            jax.ShapeDtypeStruct((rest, BLOCK), jnp.bfloat16),
        ),
        grid_spec=pltpu.PrefetchScalarGridSpec(
            num_scalar_prefetch=1,
            grid=(batches,),
            in_specs=passage_specs + [w_spec],
            out_specs=(any_spec, any_spec),
            scratch_shapes=[buf_shape, sems],
        ),
        compiler_params=pltpu.CompilerParams(vmem_limit_bytes=limit),
        cost_estimate=pl.CostEstimate(
            flops=flops, bytes_accessed=16 * 1024 * 1024, transcendentals=0
        ),
        name="forward",
    )(tab, *([rows_all] * OWN_SLOTS), w_blocks)

    def exchange(packed, first_row):
        mine = lax.psum_scatter(packed, "dp", scatter_dimension=0, tiled=True)
        height = packed.shape[0] // parts
        tiles = height // TILE
        places = tile_table(table, (first_row + rank * height) // TILE, tiles)
        slope_mine, pooled = pl.pallas_call(
            functools.partial(activate_kernel, tiles),
            out_shape=(
                jax.ShapeDtypeStruct((height, BLOCK), jnp.bfloat16),
                jax.ShapeDtypeStruct((slots * SLOT_BLOCKS, BLOCK), jnp.float32),
            ),
            in_specs=[smem, vmem, vmem, vmem],
            out_specs=(vmem, vmem),
            name="activate",
        )(places, mine, bias_rows, cot_rows)
        return lax.all_gather(slope_mine, "dp", axis=0, tiled=True), pooled

    slopes, pooled = exchange(main, 0)
    slopes_over, pooled_over = lax.cond(
        most > cap,
        lambda packed: exchange(packed, cap),
        lambda packed: (jnp.zeros_like(packed), jnp.zeros_like(pooled)),
        over,
    )
    pooled = pooled + pooled_over

    grads_all = pl.pallas_call(
        functools.partial(hidden_grad_kernel, cap),
        out_shape=jax.ShapeDtypeStruct((batches * per_batch, plen, dslice), jnp.bfloat16),
        grid_spec=pltpu.PrefetchScalarGridSpec(
            num_scalar_prefetch=1,
            grid=(batches,),
            in_specs=[any_spec, any_spec, w_spec],
            out_specs=pl.BlockSpec((per_batch, plen, dslice), lambda i, t: (i, 0, 0)),
            scratch_shapes=[buf_shape, sems],
        ),
        compiler_params=pltpu.CompilerParams(vmem_limit_bytes=limit),
        cost_estimate=pl.CostEstimate(
            flops=flops, bytes_accessed=24 * 1024 * 1024, transcendentals=0
        ),
        name="hidden_grad",
    )(tab, slopes, slopes_over, w_blocks)
    grad_hidden = lax.psum_scatter(grads_all, "vocab", scatter_dimension=0, tiled=True)

    pooled_parts = lax.all_to_all(
        pooled.reshape(parts, -1, BLOCK), "dp", split_axis=0, concat_axis=0, tiled=True
    )
    reps = jnp.sum(pooled_parts, axis=0).reshape(1, 1, OWN_SLOTS, col_width)

    group = 4
    moment_spec = pl.BlockSpec(
        (group, BLOCK, dslice), lambda i, t: (jnp.maximum(i - batches, 0), 0, 0)
    )
    moment_shape = jax.ShapeDtypeStruct((OWN_BLOCKS, BLOCK, dslice), jnp.bfloat16)
    new_first, new_second = pl.pallas_call(
        functools.partial(weight_grad_kernel, cap, batches),
        out_shape=(moment_shape, moment_shape),
        grid_spec=pltpu.PrefetchScalarGridSpec(
            num_scalar_prefetch=1,
            grid=(batches + OWN_BLOCKS // group,),
            in_specs=passage_specs + [any_spec, any_spec, moment_spec, moment_spec],
            out_specs=(moment_spec, moment_spec),
            scratch_shapes=[buf_shape, pltpu.VMEM((OWN_BLOCKS, BLOCK, dslice), jnp.float32), sems],
        ),
        compiler_params=pltpu.CompilerParams(vmem_limit_bytes=limit),
        cost_estimate=pl.CostEstimate(
            flops=flops, bytes_accessed=24 * 1024 * 1024, transcendentals=0
        ),
        name="weight_grad",
    )(
        tab,
        *([rows_all] * OWN_SLOTS),
        slopes,
        slopes_over,
        first_moment.reshape(moment_shape.shape),
        second_moment.reshape(moment_shape.shape),
    )
    return (
        reps,
        grad_hidden,
        new_first.reshape(first_moment.shape),
        new_second.reshape(second_moment.shape),
    )


def solution(mesh):
    return jax.shard_map(
        shards,
        mesh=mesh,
        in_specs=(
            P("vocab", None, "dp"),
            P("vocab", "dp"),
            P("vocab"),
            P("vocab", "dp"),
            P("vocab", "dp"),
            P(None, "vocab", None),
            P(None, "vocab", None),
            P(),
            P(),
        ),
        out_specs=(
            P("dp", "vocab", None, None),
            P("vocab", None, "dp"),
            P("vocab", "dp"),
            P("vocab", "dp"),
        ),
        check_vma=False,
    )
```

```python
import functools

import jax
import jax.numpy as jnp
from jax import lax
from jax.experimental import pallas as pl
from jax.experimental.pallas import tpu as pltpu
from jax.sharding import PartitionSpec as P

BLOCK = 128
OWN_BLOCKS = 32
SLOT_BLOCKS = 4
OWN_SLOTS = 4
TILE = 16
RING = 4
CAP_SHARE = 15
CAP_PARTS = 32

beta_one = 0.9
beta_two = 0.999

PASS, COUNT, ROWS, OFF, LEN, IDS = 0, 1, 2, 3, 4, 5
WIDTH = 16
UNIT, START, TLEN, BIAS_ROW, COT_ROW = 0, 1, 2, 3, 4
TWIDTH = 8

CONTRACT_LAST = (((1,), (1,)), ((), ()))
CONTRACT_FIRST = (((0,), (0,)), ((), ()))


def slot_table(counts_all, ids, lengths, me):
    batches, per_batch, owners = counts_all.shape
    live = (counts_all > 0).astype(jnp.int32)
    place = jnp.arange(per_batch, dtype=jnp.int32)
    earlier = (place[None, :] < place[:, None]).astype(jnp.int32)
    rank = jnp.sum(live[:, None, :, :] * earlier[None, :, :, None], axis=2)
    slot_place = jnp.arange(OWN_SLOTS, dtype=jnp.int32)
    padded = (lengths + TILE - 1) // TILE * TILE
    kept = live * (rank < OWN_SLOTS)
    totals = jnp.sum(kept * counts_all * padded[:, :, None], axis=(0, 1))
    counts = lax.dynamic_index_in_dim(counts_all, me, 2, keepdims=False)
    live_me = lax.dynamic_index_in_dim(live, me, 2, keepdims=False)
    rank_me = lax.dynamic_index_in_dim(rank, me, 2, keepdims=False)
    chosen = (
        (live_me[:, None, :] == 1) & (rank_me[:, None, :] == slot_place[None, :, None])
    ).astype(jnp.int32)
    first = jnp.arange(batches, dtype=jnp.int32)[:, None] * per_batch
    passage = jnp.sum(chosen * place[None, None, :], axis=2) + first
    count = jnp.sum(chosen * counts[:, None, :], axis=2)
    length = jnp.sum(chosen * lengths[:, None, :], axis=2)
    rows = jnp.sum(chosen * padded[:, None, :], axis=2)
    slot_ids = jnp.sum(chosen[:, :, :, None] * ids[:, None, :, :], axis=2)
    slots = batches * OWN_SLOTS
    need = (count * rows).reshape(slots)
    order = jnp.arange(slots, dtype=jnp.int32)
    off = jnp.sum(jnp.where(order[None, :] < order[:, None], need[None, :], 0), axis=1)
    columns = [
        passage.reshape(slots, 1),
        count.reshape(slots, 1),
        rows.reshape(slots, 1),
        off.reshape(slots, 1),
        length.reshape(slots, 1),
        slot_ids.reshape(slots, SLOT_BLOCKS),
        jnp.zeros((slots, WIDTH - IDS - SLOT_BLOCKS), jnp.int32),
    ]
    return jnp.concatenate(columns, axis=1), jnp.max(totals)


def tile_table(slots, first_tile, tiles):
    at = first_tile + jnp.arange(tiles, dtype=jnp.int32)
    starts = slots[:, OFF] // TILE
    holder = jnp.sum((starts[None, :] <= at[:, None]).astype(jnp.int32), axis=1) - 1
    order = jnp.arange(slots.shape[0], dtype=jnp.int32)
    pick = (holder[:, None] == order[None, :]).astype(jnp.int32)
    mine = jnp.sum(pick[:, :, None] * slots[None, :, :], axis=1)
    height = mine[:, ROWS] // TILE
    rel = at - mine[:, OFF] // TILE
    q = sum((rel >= height * n).astype(jnp.int32) for n in range(1, SLOT_BLOCKS))
    start = (rel - q * height) * TILE
    length = jnp.where(rel < height * mine[:, COUNT], mine[:, LEN], 0)
    which = jnp.arange(SLOT_BLOCKS, dtype=jnp.int32)
    block = jnp.sum(
        jnp.where(which[None, :] == q[:, None], mine[:, IDS : IDS + SLOT_BLOCKS], 0), axis=1
    )
    columns = [
        holder * SLOT_BLOCKS + q,
        start,
        length,
        block,
        mine[:, PASS] * SLOT_BLOCKS + q,
    ]
    filler = jnp.zeros((tiles,), jnp.int32)
    return jnp.stack(columns + [filler] * (TWIDTH - len(columns)), axis=1).reshape(-1)


def slot_weights(w_ref, tab_ref, base):
    return jnp.concatenate([w_ref[tab_ref[base + IDS + q]] for q in range(SLOT_BLOCKS)], axis=0)


def slot_slopes(buf, tab_ref, base):
    plen = BLOCK
    count, rows = tab_ref[base + COUNT], tab_ref[base + ROWS]
    off, length = tab_ref[base + OFF], tab_ref[base + LEN]
    token = lax.broadcasted_iota(jnp.int32, (plen, BLOCK), 0)
    pieces = []
    for q in range(SLOT_BLOCKS):
        at = pl.multiple_of(off + q * rows, TILE)
        value = buf[pl.ds(at, plen), :]
        bound = jnp.where(q < count, length, 0)
        pieces.append(jnp.where(token < bound, value.astype(jnp.float32), 0.0).astype(jnp.bfloat16))
    return jnp.concatenate(pieces, axis=1)


def placed(tab_ref, slots, buf, pieces, sems, out):
    ahead, across = pieces[:RING], pieces[RING:]
    half = ahead[0].shape[1]
    base = slots * WIDTH
    x, y = tab_ref[base], tab_ref[base + 1]
    copies = []
    for dx in range(RING):
        for dy in range(RING):
            if out:
                to_x, to_y = x + dx, y + dy
            else:
                to_x, to_y = x - dx + RING, y - dy + RING
            owner = lax.rem(to_y, RING) * RING + lax.rem(to_x, RING)
            start = pl.multiple_of(owner * (2 * half), TILE)
            if out:
                first, second = ahead[dx].at[dy], across[dy].at[dx]
            else:
                first, second = ahead[dy].at[dx], across[dx].at[dy]
            for ref, at in ((first, start), (second, pl.multiple_of(start + half, TILE))):
                view = buf.at[pl.ds(at, half)]
                source, target = (view, ref) if out else (ref, view)
                copies.append(pltpu.make_async_copy(source, target, sems.at[len(copies)]))
    return copies


def packed_total(tab_ref, slots):
    base = (slots - 1) * WIDTH
    return tab_ref[base + OFF] + tab_ref[base + COUNT] * tab_ref[base + ROWS]


def forward_kernel(cap, tab_ref, *refs):
    hidden_refs, w_ref = refs[:OWN_SLOTS], refs[OWN_SLOTS]
    pieces = refs[OWN_SLOTS + 1 : OWN_SLOTS + 1 + 2 * RING]
    rest_ref, buf, sems = refs[OWN_SLOTS + 1 + 2 * RING :]
    j = pl.program_id(0)
    slots = pl.num_programs(0) * OWN_SLOTS
    for s in range(OWN_SLOTS):
        base = (j * OWN_SLOTS + s) * WIDTH
        count, rows, off = tab_ref[base + COUNT], tab_ref[base + ROWS], tab_ref[base + OFF]

        @pl.when(count > 0)
        def _():
            value = lax.dot_general(
                hidden_refs[s][0],
                slot_weights(w_ref, tab_ref, base),
                CONTRACT_LAST,
                preferred_element_type=jnp.float32,
            ).astype(jnp.bfloat16)
            for q in range(SLOT_BLOCKS):
                at = pl.multiple_of(off + q * rows, TILE)
                buf[pl.ds(at, BLOCK), :] = value[:, q * BLOCK : (q + 1) * BLOCK]

    @pl.when(j == pl.num_programs(0) - 1)
    def _():
        copies = placed(tab_ref, slots, buf, pieces, sems, True)
        for copy in copies:
            copy.start()
        for copy in copies:
            copy.wait()

        @pl.when(packed_total(tab_ref, slots) > cap)
        def _():
            more = pltpu.make_async_copy(
                buf.at[pl.ds(cap, rest_ref.shape[0])], rest_ref, sems.at[0]
            )
            more.start()
            more.wait()


def activate_kernel(tiles, tile_ref, bias_ref, cot_ref, *refs):
    lg_refs, (slope_ref, pooled_ref) = refs[:-2], refs[-2:]
    pooled_ref[...] = jnp.zeros_like(pooled_ref)

    def step(i, carry):
        base = i * TWIDTH
        unit, start = tile_ref[base + UNIT], tile_ref[base + START]
        length, bias_row = tile_ref[base + TLEN], tile_ref[base + BIAS_ROW]
        cot_row = tile_ref[base + COT_ROW]
        at = pl.multiple_of(i * TILE, TILE)
        x = bias_ref[pl.ds(bias_row, 1), :]
        for lg_ref in lg_refs:
            x = x + lg_ref[pl.ds(at, TILE), :].astype(jnp.float32)
        token = lax.broadcasted_iota(jnp.int32, x.shape, 0) + start
        keep = token < length
        divisor = jnp.full((1, BLOCK), jnp.maximum(length, 1), jnp.int32).astype(jnp.float32)
        weight = 1.0 / divisor
        small = jnp.exp(-jnp.abs(x))
        soft = jnp.maximum(x, 0.0) + jnp.log1p(small)
        sig = jnp.where(x >= 0, 1.0, small) / (1.0 + small)
        gain = jnp.where(keep, jnp.log1p(soft) * weight, 0.0)
        pooled_ref[pl.ds(unit, 1), :] += jnp.sum(gain, axis=0, keepdims=True)
        cot = cot_ref[pl.ds(cot_row, 1), :] * weight
        slope = jnp.where(keep, cot * sig / (1.0 + soft), 0.0)
        slope_ref[pl.ds(at, TILE), :] = slope.astype(jnp.bfloat16)
        return carry

    lax.fori_loop(0, tiles, step, 0, unroll=4)


def load_slopes(cap, tab_ref, pieces, rest_ref, buf, sems, slots):
    copies = placed(tab_ref, slots, buf, pieces, sems, False)
    for copy in copies:
        copy.start()
    for copy in copies:
        copy.wait()

    @pl.when(packed_total(tab_ref, slots) > cap)
    def _():
        more = pltpu.make_async_copy(rest_ref, buf.at[pl.ds(cap, rest_ref.shape[0])], sems.at[0])
        more.start()
        more.wait()


def hidden_grad_kernel(cap, tab_ref, *refs):
    pieces = refs[: 2 * RING]
    rest_ref, w_ref, out_ref, buf, sems = refs[2 * RING :]
    j = pl.program_id(0)

    @pl.when(j == 0)
    def _():
        load_slopes(cap, tab_ref, pieces, rest_ref, buf, sems, pl.num_programs(0) * OWN_SLOTS)

    out_ref[...] = jnp.zeros_like(out_ref)
    per_batch = out_ref.shape[0]
    for s in range(OWN_SLOTS):
        base = (j * OWN_SLOTS + s) * WIDTH
        local = tab_ref[base + PASS] - j * per_batch

        @pl.when(tab_ref[base + COUNT] > 0)
        def _():
            value = jnp.dot(
                slot_slopes(buf, tab_ref, base),
                slot_weights(w_ref, tab_ref, base),
                preferred_element_type=jnp.float32,
            )
            out_ref[local] = value.astype(jnp.bfloat16)


def weight_grad_kernel(cap, batches, tab_ref, *refs):
    hidden_refs, pieces = refs[:OWN_SLOTS], refs[OWN_SLOTS : OWN_SLOTS + 2 * RING]
    rest_ref, m_ref, v_ref, first_ref, second_ref, buf, acc, sems = refs[OWN_SLOTS + 2 * RING :]
    i = pl.program_id(0)

    @pl.when(i == 0)
    def _():
        load_slopes(cap, tab_ref, pieces, rest_ref, buf, sems, batches * OWN_SLOTS)
        acc[...] = jnp.zeros_like(acc)

    @pl.when(i < batches)
    def _():
        for s in range(OWN_SLOTS):
            base = (i * OWN_SLOTS + s) * WIDTH

            @pl.when(tab_ref[base + COUNT] > 0)
            def _():
                value = lax.dot_general(
                    slot_slopes(buf, tab_ref, base),
                    hidden_refs[s][0],
                    CONTRACT_FIRST,
                    preferred_element_type=jnp.float32,
                )
                for q in range(SLOT_BLOCKS):
                    acc[tab_ref[base + IDS + q]] += value[q * BLOCK : (q + 1) * BLOCK]

    @pl.when(i >= batches)
    def _():
        group = m_ref.shape[0]
        at = (i - batches) * group
        grad = acc[pl.ds(at, group)]
        m = m_ref[...].astype(jnp.float32)
        v = v_ref[...].astype(jnp.float32)
        first_ref[...] = (beta_one * m + (1.0 - beta_one) * grad).astype(jnp.bfloat16)
        second_ref[...] = (beta_two * v + (1.0 - beta_two) * grad * grad).astype(jnp.bfloat16)


def shards(
    hidden,
    weights,
    bias,
    first_moment,
    second_moment,
    rep_cot,
    active_blocks,
    block_counts,
    passage_len,
):
    batches = lax.axis_size("vocab")
    parts = lax.axis_size("dp")
    per_batch, plen, dslice = hidden.shape
    col_width = SLOT_BLOCKS * BLOCK
    slots = batches * OWN_SLOTS
    full = slots * SLOT_BLOCKS * plen
    cap = full * CAP_SHARE // CAP_PARTS
    rest = full - cap
    slack = 2 * BLOCK
    me = lax.axis_index("vocab")
    rank = lax.axis_index("dp")

    rows_all = lax.all_gather(hidden, "vocab", axis=0, tiled=True)

    table, most = slot_table(
        block_counts.reshape(batches, per_batch, batches),
        active_blocks.reshape(batches, per_batch, SLOT_BLOCKS),
        passage_len.reshape(batches, per_batch),
        me,
    )
    place = jnp.where(
        jnp.arange(WIDTH) == 0, lax.rem(rank, RING), jnp.where(jnp.arange(WIDTH) == 1, rank // RING, 0)
    )
    tab = jnp.concatenate([table.reshape(-1), place.astype(jnp.int32)])
    cot_rows = rep_cot.astype(jnp.float32).reshape(-1, BLOCK)
    bias_rows = bias.reshape(OWN_BLOCKS, BLOCK)
    w_blocks = weights.reshape(OWN_BLOCKS, BLOCK, dslice)

    any_spec = pl.BlockSpec(memory_space=pl.ANY)
    vmem = pl.BlockSpec(memory_space=pltpu.VMEM)
    smem = pl.BlockSpec(memory_space=pltpu.SMEM)

    def passage_spec(s):
        def index(i, t):
            row = jnp.minimum(i, batches - 1) * OWN_SLOTS + s
            return (t[row * WIDTH + PASS], 0, 0)

        return pl.BlockSpec((1, plen, dslice), index)

    passage_specs = [passage_spec(s) for s in range(OWN_SLOTS)]
    w_spec = pl.BlockSpec(
        w_blocks.shape, lambda i, t: (0, 0, 0), pipeline_mode=pl.Buffered(buffer_count=1)
    )
    buf_shape = pltpu.VMEM((full + slack, BLOCK), jnp.bfloat16)
    sems = pltpu.SemaphoreType.DMA((2 * parts,))
    half = cap // parts // 2
    piece = jax.ShapeDtypeStruct((RING, half, BLOCK), jnp.bfloat16)
    limit = 60 * 1024 * 1024
    flops = 2 * slots * plen * col_width * dslice

    *partials, over = pl.pallas_call(
        functools.partial(forward_kernel, cap),
        out_shape=(*[piece] * (2 * RING), jax.ShapeDtypeStruct((rest, BLOCK), jnp.bfloat16)),
        grid_spec=pltpu.PrefetchScalarGridSpec(
            num_scalar_prefetch=1,
            grid=(batches,),
            in_specs=passage_specs + [w_spec],
            out_specs=(any_spec,) * (2 * RING + 1),
            scratch_shapes=[buf_shape, sems],
        ),
        compiler_params=pltpu.CompilerParams(vmem_limit_bytes=limit),
        cost_estimate=pl.CostEstimate(
            flops=flops, bytes_accessed=16 * 1024 * 1024, transcendentals=0
        ),
        name="forward",
    )(tab, *([rows_all] * OWN_SLOTS), w_blocks)

    def activate(places, terms):
        height = terms[0].shape[0]
        return pl.pallas_call(
            functools.partial(activate_kernel, height // TILE),
            out_shape=(
                jax.ShapeDtypeStruct((height, BLOCK), jnp.bfloat16),
                jax.ShapeDtypeStruct((slots * SLOT_BLOCKS, BLOCK), jnp.float32),
            ),
            in_specs=[smem] + [vmem] * (2 + len(terms)),
            out_specs=(vmem, vmem),
            name="activate",
        )(places, bias_rows, cot_rows, *terms)

    def move(value, axis, step):
        pairs = []
        for y in range(RING):
            for x in range(RING):
                to_x, to_y = ((x + step) % RING, y) if axis == "x" else (x, (y + step) % RING)
                pairs.append((y * RING + x, to_y * RING + to_x))
        return lax.ppermute(value, "dp", pairs)

    steps = (1, 3, 2)

    def first_stage(terms, axis):
        arrived = [move(terms[d], axis, d) for d in steps]
        total = terms[0].astype(jnp.float32)
        for value in arrived:
            total = total + value.astype(jnp.float32)
        return total.astype(jnp.bfloat16)

    def second_stage(summed, axis):
        return [summed[0]] + [move(summed[d], axis, d) for d in steps]

    def spread(value, axis):
        arrived = {d: move(value, axis, d) for d in steps}
        return [value] + [arrived[d] for d in range(1, RING)]

    sum_a = first_stage(partials[:RING], "x")
    sum_b = first_stage(partials[RING:], "y")
    terms_a = second_stage(sum_a, "y")
    terms_b = second_stage(sum_b, "x")
    first = rank * 2 * half // TILE
    slope_a, pooled_a = activate(tile_table(table, first, half // TILE), terms_a)
    slope_b, pooled_b = activate(tile_table(table, first + half // TILE, half // TILE), terms_b)
    row_a = jnp.stack(spread(slope_a, "x"))
    column_b = jnp.stack(spread(slope_b, "y"))
    slopes = spread(row_a, "y") + spread(column_b, "x")
    pooled = pooled_a + pooled_b

    def exchange(packed):
        mine = lax.psum_scatter(packed, "dp", scatter_dimension=0, tiled=True)
        height = packed.shape[0] // parts
        places = tile_table(table, (cap + rank * height) // TILE, height // TILE)
        slope_mine, pooled_mine = activate(places, [mine])
        return lax.all_gather(slope_mine, "dp", axis=0, tiled=True), pooled_mine

    slopes_over, pooled_over = lax.cond(
        most > cap,
        exchange,
        lambda packed: (jnp.zeros_like(packed), jnp.zeros_like(pooled)),
        over,
    )
    pooled = pooled + pooled_over

    grads_all = pl.pallas_call(
        functools.partial(hidden_grad_kernel, cap),
        out_shape=jax.ShapeDtypeStruct((batches * per_batch, plen, dslice), jnp.bfloat16),
        grid_spec=pltpu.PrefetchScalarGridSpec(
            num_scalar_prefetch=1,
            grid=(batches,),
            in_specs=[any_spec] * (2 * RING + 1) + [w_spec],
            out_specs=pl.BlockSpec((per_batch, plen, dslice), lambda i, t: (i, 0, 0)),
            scratch_shapes=[buf_shape, sems],
        ),
        compiler_params=pltpu.CompilerParams(vmem_limit_bytes=limit),
        cost_estimate=pl.CostEstimate(
            flops=flops, bytes_accessed=24 * 1024 * 1024, transcendentals=0
        ),
        name="hidden_grad",
    )(tab, *slopes, slopes_over, w_blocks)
    grad_hidden = lax.psum_scatter(grads_all, "vocab", scatter_dimension=0, tiled=True)

    pooled_parts = lax.all_to_all(
        pooled.reshape(parts, -1, BLOCK), "dp", split_axis=0, concat_axis=0, tiled=True
    )
    reps = jnp.sum(pooled_parts, axis=0).reshape(1, 1, OWN_SLOTS, col_width)

    group = 4
    moment_spec = pl.BlockSpec(
        (group, BLOCK, dslice), lambda i, t: (jnp.maximum(i - batches, 0), 0, 0)
    )
    moment_shape = jax.ShapeDtypeStruct((OWN_BLOCKS, BLOCK, dslice), jnp.bfloat16)
    new_first, new_second = pl.pallas_call(
        functools.partial(weight_grad_kernel, cap, batches),
        out_shape=(moment_shape, moment_shape),
        grid_spec=pltpu.PrefetchScalarGridSpec(
            num_scalar_prefetch=1,
            grid=(batches + OWN_BLOCKS // group,),
            in_specs=passage_specs + [any_spec] * (2 * RING + 1) + [moment_spec] * 2,
            out_specs=(moment_spec, moment_spec),
            scratch_shapes=[buf_shape, pltpu.VMEM((OWN_BLOCKS, BLOCK, dslice), jnp.float32), sems],
        ),
        compiler_params=pltpu.CompilerParams(vmem_limit_bytes=limit),
        cost_estimate=pl.CostEstimate(
            flops=flops, bytes_accessed=24 * 1024 * 1024, transcendentals=0
        ),
        name="weight_grad",
    )(
        tab,
        *([rows_all] * OWN_SLOTS),
        *slopes,
        slopes_over,
        first_moment.reshape(moment_shape.shape),
        second_moment.reshape(moment_shape.shape),
    )
    return (
        reps,
        grad_hidden,
        new_first.reshape(first_moment.shape),
        new_second.reshape(second_moment.shape),
    )


def solution(mesh):
    return jax.shard_map(
        shards,
        mesh=mesh,
        in_specs=(
            P("vocab", None, "dp"),
            P("vocab", "dp"),
            P("vocab"),
            P("vocab", "dp"),
            P("vocab", "dp"),
            P(None, "vocab", None),
            P(None, "vocab", None),
            P(),
            P(),
        ),
        out_specs=(
            P("dp", "vocab", None, None),
            P("vocab", None, "dp"),
            P("vocab", "dp"),
            P("vocab", "dp"),
        ),
        check_vma=False,
    )
```

```python
import functools

import jax
import jax.numpy as jnp
from jax import lax
from jax.experimental import pallas as pl
from jax.experimental.pallas import tpu as pltpu
from jax.sharding import PartitionSpec as P

BLOCK = 128
OWN_BLOCKS = 32
SLOT_BLOCKS = 4
OWN_SLOTS = 4
TILE = 16
RING = 4
CHIPS = 8
UNIT_ROWS = SLOT_BLOCKS * OWN_SLOTS * BLOCK
GROUPS = (((0, 1, 2), 10752), ((3, 4), 7168))

beta_one = 0.9
beta_two = 0.999

PASS, COUNT, ROWS, OFF, LEN, IDS, GLOBAL, FIRST = 0, 1, 2, 3, 4, 5, 9, 10
WIDTH = 16
UNIT, START, TLEN, BIAS_ROW, COT_ROW = 0, 1, 2, 3, 4
TWIDTH = 8

CONTRACT_LAST = (((1,), (1,)), ((), ()))
CONTRACT_FIRST = (((0,), (0,)), ((), ()))
LIMIT = 60 * 1024 * 1024


def positions(rounds):
    out = []
    for r in rounds:
        if r == 0:
            out += [(0, True), (0, False)]
        elif 2 * r == CHIPS:
            out += [(r, True), (r, False)]
        else:
            out += [(-r, True), (r, True), (-r, False), (r, False)]
    return out


def device_at(chip, core, step, same):
    return lax.rem(chip + step + CHIPS, CHIPS) * 2 + (core if same else 1 - core)


def reorder(rows, order):
    pick = order[:, None] == jnp.arange(rows.shape[0], dtype=jnp.int32)[None, :]
    pick = pick.reshape(pick.shape + (1,) * (rows.ndim - 1))
    return jnp.sum(jnp.where(pick, rows[None], 0), axis=1)


def slot_columns(counts_all, ids, lengths, me):
    batches, per_batch, owners = counts_all.shape
    live = (counts_all > 0).astype(jnp.int32)
    place = jnp.arange(per_batch, dtype=jnp.int32)
    earlier = (place[None, :] < place[:, None]).astype(jnp.int32)
    rank = jnp.sum(live[:, None, :, :] * earlier[None, :, :, None], axis=2)
    slot_place = jnp.arange(OWN_SLOTS, dtype=jnp.int32)
    padded = (lengths + TILE - 1) // TILE * TILE
    needed = jnp.sum(counts_all * padded[:, :, None], axis=1)
    counts = lax.dynamic_index_in_dim(counts_all, me, 2, keepdims=False)
    live_me = lax.dynamic_index_in_dim(live, me, 2, keepdims=False)
    rank_me = lax.dynamic_index_in_dim(rank, me, 2, keepdims=False)
    chosen = (
        (live_me[:, None, :] == 1) & (rank_me[:, None, :] == slot_place[None, :, None])
    ).astype(jnp.int32)
    passage = jnp.sum(chosen * place[None, None, :], axis=2)
    count = jnp.sum(chosen * counts[:, None, :], axis=2)
    length = jnp.sum(chosen * lengths[:, None, :], axis=2)
    rows = jnp.sum(chosen * padded[:, None, :], axis=2)
    slot_ids = jnp.sum(chosen[:, :, :, None] * ids[:, None, :, :], axis=2)
    batch = jnp.arange(batches, dtype=jnp.int32)[:, None]
    base = jnp.stack(
        [passage, count, rows, jnp.zeros_like(rows), length]
        + [slot_ids[:, :, q] for q in range(SLOT_BLOCKS)]
        + [
            batch * per_batch + passage,
            (batch * OWN_SLOTS + slot_place[None, :]) * SLOT_BLOCKS,
        ],
        axis=2,
    )
    base = jnp.pad(base, ((0, 0), (0, 0), (0, WIDTH - base.shape[2])))
    live_home = lax.dynamic_index_in_dim(live, me, 0, keepdims=False)
    rank_home = lax.dynamic_index_in_dim(rank, me, 0, keepdims=False)
    at_home = (live_home[:, :, None] == 1) & (rank_home[:, :, None] == slot_place[None, None, :])
    home = jnp.sum(jnp.where(at_home, place[:, None, None] + 1, 0), axis=0) - 1
    return base, home, needed


def group_table(base, order):
    rows = reorder(base, order).reshape(-1, WIDTH)
    slots = rows.shape[0]
    line = jnp.arange(slots, dtype=jnp.int32)
    need = rows[:, COUNT] * rows[:, ROWS]
    off = jnp.sum(jnp.where(line[None, :] < line[:, None], need[None, :], 0), axis=1)
    column = jnp.arange(WIDTH, dtype=jnp.int32) == OFF
    return jnp.where(column[None, :], off[:, None], rows)


def tile_table(slots, first_tile, tiles):
    at = first_tile + jnp.arange(tiles, dtype=jnp.int32)
    starts = slots[:, OFF] // TILE
    holder = jnp.sum((starts[None, :] <= at[:, None]).astype(jnp.int32), axis=1) - 1
    mine = reorder(slots, holder)
    height = mine[:, ROWS] // TILE
    rel = at - mine[:, OFF] // TILE
    q = sum((rel >= height * n).astype(jnp.int32) for n in range(1, SLOT_BLOCKS))
    start = (rel - q * height) * TILE
    length = jnp.where(rel < height * mine[:, COUNT], mine[:, LEN], 0)
    which = jnp.arange(SLOT_BLOCKS, dtype=jnp.int32)
    block = jnp.sum(
        jnp.where(which[None, :] == q[:, None], mine[:, IDS : IDS + SLOT_BLOCKS], 0), axis=1
    )
    columns = [mine[:, FIRST] + q, start, length, block, mine[:, GLOBAL] * SLOT_BLOCKS + q]
    filler = jnp.zeros((tiles,), jnp.int32)
    return jnp.stack(columns + [filler] * (TWIDTH - len(columns)), axis=1).reshape(-1)


def slot_weights(w_ref, tab_ref, base):
    return jnp.concatenate([w_ref[tab_ref[base + IDS + q]] for q in range(SLOT_BLOCKS)], axis=0)


def slot_slopes(buf, tab_ref, base, shift):
    count, rows = tab_ref[base + COUNT], tab_ref[base + ROWS]
    off, length = tab_ref[base + OFF] + shift, tab_ref[base + LEN]
    token = lax.broadcasted_iota(jnp.int32, (BLOCK, BLOCK), 0)
    pieces = []
    for q in range(SLOT_BLOCKS):
        at = pl.multiple_of(off + q * rows, TILE)
        value = buf[pl.ds(at, BLOCK), :]
        bound = jnp.where(q < count, length, 0)
        pieces.append(jnp.where(token < bound, value.astype(jnp.float32), 0.0).astype(jnp.bfloat16))
    return jnp.concatenate(pieces, axis=1)


def placed(tab_ref, slots, buf, shift, pieces, sems, first_sem, out):
    ahead, across = pieces[:RING], pieces[RING:]
    half = ahead[0].shape[1]
    x, y = tab_ref[slots * WIDTH], tab_ref[slots * WIDTH + 1]
    copies = []
    for dx in range(RING):
        for dy in range(RING):
            if out:
                to_x, to_y = x + dx, y + dy
                first, second = ahead[dx].at[dy], across[dy].at[dx]
            else:
                to_x, to_y = x - dx + RING, y - dy + RING
                first, second = ahead[dy].at[dx], across[dx].at[dy]
            owner = lax.rem(to_y, RING) * RING + lax.rem(to_x, RING)
            start = owner * (2 * half) + shift
            for ref, at in ((first, start), (second, start + half)):
                view = buf.at[pl.ds(pl.multiple_of(at, TILE), half)]
                source, target = (view, ref) if out else (ref, view)
                sem = sems.at[first_sem + len(copies)]
                copies.append(pltpu.make_async_copy(source, target, sem))
    return copies


def packed_total(tab_ref, slots):
    base = (slots - 1) * WIDTH
    return tab_ref[base + OFF] + tab_ref[base + COUNT] * tab_ref[base + ROWS]


def fetch_passages(tab_ref, hidden_refs, hbuf, first, hsems):
    for i, ref in enumerate(hidden_refs):
        for s in range(OWN_SLOTS):
            at = i * OWN_SLOTS + s
            row = ref.at[tab_ref[at * WIDTH + PASS]]
            pltpu.make_async_copy(row, hbuf.at[first + at], hsems.at[first + at]).start()


def forward_kernel(cap, n, tab_ref, *refs):
    hidden_refs, w_ref, pieces = refs[:n], refs[n], refs[n + 1 : n + 1 + 2 * RING]
    rest_ref, hbuf, buf, hsems, sems = refs[n + 1 + 2 * RING :]
    slots = n * OWN_SLOTS
    fetch_passages(tab_ref, hidden_refs, hbuf, 0, hsems)

    def step(t, carry):
        base = t * WIDTH
        rows, off = tab_ref[base + ROWS], tab_ref[base + OFF]
        pltpu.make_async_copy(hidden_refs[0].at[0], hbuf.at[t], hsems.at[t]).wait()

        @pl.when(tab_ref[base + COUNT] > 0)
        def _():
            value = lax.dot_general(
                hbuf[t],
                slot_weights(w_ref, tab_ref, base),
                CONTRACT_LAST,
                preferred_element_type=jnp.float32,
            ).astype(jnp.bfloat16)
            for q in range(SLOT_BLOCKS):
                at = pl.multiple_of(off + q * rows, TILE)
                buf[pl.ds(at, BLOCK), :] = value[:, q * BLOCK : (q + 1) * BLOCK]

        return carry

    lax.fori_loop(0, slots, step, 0)
    copies = placed(tab_ref, slots, buf, 0, pieces, sems, 0, True)
    for copy in copies:
        copy.start()
    for copy in copies:
        copy.wait()

    @pl.when(packed_total(tab_ref, slots) > cap)
    def _():
        more = pltpu.make_async_copy(buf.at[pl.ds(cap, rest_ref.shape[0])], rest_ref, sems.at[0])
        more.start()
        more.wait()


def activate_kernel(tiles, tile_ref, bias_ref, cot_ref, *refs):
    lg_refs, (slope_ref, pooled_ref) = refs[:-2], refs[-2:]
    pooled_ref[...] = jnp.zeros_like(pooled_ref)

    def step(i, carry):
        base = i * TWIDTH
        unit, start = tile_ref[base + UNIT], tile_ref[base + START]
        length, bias_row = tile_ref[base + TLEN], tile_ref[base + BIAS_ROW]
        cot_row = tile_ref[base + COT_ROW]
        at = pl.multiple_of(i * TILE, TILE)
        x = bias_ref[pl.ds(bias_row, 1), :]
        for lg_ref in lg_refs:
            x = x + lg_ref[pl.ds(at, TILE), :].astype(jnp.float32)
        token = lax.broadcasted_iota(jnp.int32, x.shape, 0) + start
        keep = token < length
        divisor = jnp.full((1, BLOCK), jnp.maximum(length, 1), jnp.int32).astype(jnp.float32)
        weight = 1.0 / divisor
        small = jnp.exp(-jnp.abs(x))
        soft = jnp.maximum(x, 0.0) + jnp.log1p(small)
        sig = jnp.where(x >= 0, 1.0, small) / (1.0 + small)
        gain = jnp.where(keep, jnp.log1p(soft) * weight, 0.0)
        pooled_ref[pl.ds(unit, 1), :] += jnp.sum(gain, axis=0, keepdims=True)
        cot = cot_ref[pl.ds(cot_row, 1), :] * weight
        slope = jnp.where(keep, cot * sig / (1.0 + soft), 0.0)
        slope_ref[pl.ds(at, TILE), :] = slope.astype(jnp.bfloat16)
        return carry

    lax.fori_loop(0, tiles, step, 0, unroll=2)


def start_slopes(cap, tab_ref, pieces, rest_ref, buf, shift, sems, first_sem, slots):
    copies = placed(tab_ref, slots, buf, shift, pieces, sems, first_sem, False)
    for copy in copies:
        copy.start()
    return copies


def finish_slopes(cap, tab_ref, copies, rest_ref, buf, shift, sems, first_sem, slots):
    for copy in copies:
        copy.wait()

    @pl.when(packed_total(tab_ref, slots) > cap)
    def _():
        view = buf.at[pl.ds(cap + shift, rest_ref.shape[0])]
        more = pltpu.make_async_copy(rest_ref, view, sems.at[first_sem])
        more.start()
        more.wait()


def hidden_grad_kernel(cap, n, tab_ref, *refs):
    pieces = refs[: 2 * RING]
    rest_ref, w_ref = refs[2 * RING : 2 * RING + 2]
    out_refs = refs[2 * RING + 2 : 2 * RING + 2 + n]
    buf, obuf, sems, osems = refs[2 * RING + 2 + n :]
    slots = n * OWN_SLOTS
    copies = start_slopes(cap, tab_ref, pieces, rest_ref, buf, 0, sems, 0, slots)
    finish_slopes(cap, tab_ref, copies, rest_ref, buf, 0, sems, 0, slots)

    def step(t, carry):
        base = t * WIDTH
        live = tab_ref[base + COUNT] > 0

        @pl.when(live)
        def _():
            value = jnp.dot(
                slot_slopes(buf, tab_ref, base, 0),
                slot_weights(w_ref, tab_ref, base),
                preferred_element_type=jnp.float32,
            )
            obuf[t] = value.astype(jnp.bfloat16)

        @pl.when(jnp.logical_not(live))
        def _():
            obuf[t] = jnp.zeros(obuf.shape[1:], jnp.bfloat16)

        return carry

    lax.fori_loop(0, slots, step, 0)
    done = [
        pltpu.make_async_copy(obuf.at[pl.ds(i * OWN_SLOTS, OWN_SLOTS)], out_refs[i], osems.at[i])
        for i in range(n)
    ]
    for copy in done:
        copy.start()
    for copy in done:
        copy.wait()


def weight_grad_kernel(groups, *refs):
    tabs, refs = refs[: len(groups)], refs[len(groups) :]
    total = sum(n for n, _, _ in groups)
    hidden_refs, refs = refs[:total], refs[total:]
    slope_refs, refs = refs[: len(groups) * (2 * RING + 1)], refs[len(groups) * (2 * RING + 1) :]
    m_ref, v_ref, first_ref, second_ref, hbuf, buf, acc, hsems, sems = refs
    plan, pos, shift = [], 0, 0
    for g, (n, cap, full) in enumerate(groups):
        mine = slope_refs[g * (2 * RING + 1) : (g + 1) * (2 * RING + 1)]
        fetch_passages(tabs[g], hidden_refs[pos : pos + n], hbuf, pos * OWN_SLOTS, hsems)
        first_sem = g * 2 * RING * RING
        copies = start_slopes(
            cap, tabs[g], mine[:-1], mine[-1], buf, shift, sems, first_sem, n * OWN_SLOTS
        )
        plan.append((copies, mine[-1], pos, shift, first_sem))
        pos, shift = pos + n, shift + full
    acc[...] = jnp.zeros_like(acc)
    for g, (n, cap, full) in enumerate(groups):
        copies, rest_ref, pos, shift, first_sem = plan[g]
        tab_ref, slots = tabs[g], n * OWN_SLOTS
        finish_slopes(cap, tab_ref, copies, rest_ref, buf, shift, sems, first_sem, slots)

        def step(t, carry, tab_ref=tab_ref, pos=pos, shift=shift):
            base = t * WIDTH
            at = pos * OWN_SLOTS + t
            pltpu.make_async_copy(hidden_refs[0].at[0], hbuf.at[at], hsems.at[at]).wait()

            @pl.when(tab_ref[base + COUNT] > 0)
            def _():
                value = lax.dot_general(
                    slot_slopes(buf, tab_ref, base, shift),
                    hbuf[at],
                    CONTRACT_FIRST,
                    preferred_element_type=jnp.float32,
                )
                for q in range(SLOT_BLOCKS):
                    acc[tab_ref[base + IDS + q]] += value[q * BLOCK : (q + 1) * BLOCK]

            return carry

        lax.fori_loop(0, slots, step, 0)

    def update(i, carry):
        grad = acc[i]
        m, v = m_ref[i].astype(jnp.float32), v_ref[i].astype(jnp.float32)
        first_ref[i] = (beta_one * m + (1.0 - beta_one) * grad).astype(jnp.bfloat16)
        second_ref[i] = (beta_two * v + (1.0 - beta_two) * grad * grad).astype(jnp.bfloat16)
        return carry

    lax.fori_loop(0, acc.shape[0], update, 0)


def gather_home_kernel(home_ref, *refs):
    terms, out_ref, acc = refs[:-2], refs[-2], refs[-1]
    acc[...] = jnp.zeros_like(acc)
    for i, term in enumerate(terms):
        for s in range(OWN_SLOTS):
            local = home_ref[i * OWN_SLOTS + s]

            @pl.when(local >= 0)
            def _():
                acc[local] += term[s].astype(jnp.float32)

    out_ref[...] = acc[...].astype(jnp.bfloat16)


def shards(
    hidden,
    weights,
    bias,
    first_moment,
    second_moment,
    rep_cot,
    active_blocks,
    block_counts,
    passage_len,
):
    batches = lax.axis_size("vocab")
    parts = lax.axis_size("dp")
    per_batch, plen, dslice = hidden.shape
    col_width = SLOT_BLOCKS * BLOCK
    me = lax.axis_index("vocab")
    chip, core = me // 2, lax.rem(me, 2)
    rank = lax.axis_index("dp")

    def along(value, step, same=True):
        pairs = []
        for z in range(CHIPS):
            for c in range(2):
                pairs.append((2 * z + c, 2 * ((z + step) % CHIPS) + (c if same else 1 - c)))
        return lax.ppermute(value, "vocab", pairs)

    held = {(0, True): hidden, (0, False): along(hidden, 0, False)}
    up = down = hidden
    for r in range(1, CHIPS // 2):
        up, down = along(up, 1), along(down, -1)
        held[(-r, True)], held[(r, True)] = up, down
        held[(-r, False)], held[(r, False)] = along(up, 0, False), along(down, 0, False)
    far = jnp.where(core == 0, up, down)
    pairs = []
    for z in range(CHIPS):
        pairs += [(2 * z, 2 * ((z + 1) % CHIPS)), (2 * z + 1, 2 * ((z - 1) % CHIPS) + 1)]
    far = lax.ppermute(far, "vocab", pairs)
    held[(CHIPS // 2, True)] = far
    held[(CHIPS // 2, False)] = along(far, 0, False)

    base, home, needed = slot_columns(
        block_counts.reshape(batches, per_batch, batches),
        active_blocks.reshape(batches, per_batch, SLOT_BLOCKS),
        passage_len.reshape(batches, per_batch),
        me,
    )
    line = jnp.arange(WIDTH)
    corner = jnp.where(line == 0, lax.rem(rank, RING), jnp.where(line == 1, rank // RING, 0))
    corner = corner.astype(jnp.int32)
    cot_rows = rep_cot.astype(jnp.float32).reshape(-1, BLOCK)
    bias_rows = bias.reshape(OWN_BLOCKS, BLOCK)
    w_blocks = weights.reshape(OWN_BLOCKS, BLOCK, dslice)
    units = batches * OWN_SLOTS * SLOT_BLOCKS

    any_spec = pl.BlockSpec(memory_space=pl.ANY)
    vmem = pl.BlockSpec(memory_space=pltpu.VMEM)
    smem = pl.BlockSpec(memory_space=pltpu.SMEM)
    params = pltpu.CompilerParams(vmem_limit_bytes=LIMIT)

    def cost(n, count):
        flops = 2 * n * UNIT_ROWS * BLOCK * dslice // BLOCK
        return pl.CostEstimate(flops=flops, bytes_accessed=count * 1024 * 1024, transcendentals=0)

    def activate(places, terms):
        height = terms[0].shape[0]
        return pl.pallas_call(
            functools.partial(activate_kernel, height // TILE),
            out_shape=(
                jax.ShapeDtypeStruct((height, BLOCK), jnp.bfloat16),
                jax.ShapeDtypeStruct((units, BLOCK), jnp.float32),
            ),
            in_specs=[smem] + [vmem] * (2 + len(terms)),
            out_specs=(vmem, vmem),
            name="activate",
        )(places, bias_rows, cot_rows, *terms)

    def move(value, axis, step):
        pairs = []
        for y in range(RING):
            for x in range(RING):
                to_x, to_y = ((x + step) % RING, y) if axis == "x" else (x, (y + step) % RING)
                pairs.append((y * RING + x, to_y * RING + to_x))
        return lax.ppermute(value, "dp", pairs)

    steps = (1, 3, 2)

    def first_stage(terms, axis):
        arrived = [move(terms[d], axis, d) for d in steps]
        total = terms[0].astype(jnp.float32)
        for value in arrived:
            total = total + value.astype(jnp.float32)
        return total.astype(jnp.bfloat16)

    def second_stage(summed, axis):
        return [summed[0]] + [move(summed[d], axis, d) for d in steps]

    def spread(value, axis):
        arrived = {d: move(value, axis, d) for d in steps}
        return [value] + [arrived[d] for d in range(1, RING)]

    tabs, pooled_terms, slope_lists, back, sizes, all_held = [], [], [], {}, [], []
    for rounds, cap in GROUPS:
        where = positions(rounds)
        n = len(where)
        slots = n * OWN_SLOTS
        full = n * UNIT_ROWS
        rest, half = full - cap, cap // parts // 2
        order = jnp.stack([device_at(chip, core, step, same) for step, same in where])
        table = group_table(base, order)
        tab = jnp.concatenate([table.reshape(-1), corner])
        mine = [held[key] for key in where]
        piece = jax.ShapeDtypeStruct((RING, half, BLOCK), jnp.bfloat16)
        *partials, over = pl.pallas_call(
            functools.partial(forward_kernel, cap, n),
            out_shape=(*[piece] * (2 * RING), jax.ShapeDtypeStruct((rest, BLOCK), jnp.bfloat16)),
            in_specs=[smem] + [any_spec] * n + [vmem],
            out_specs=(any_spec,) * (2 * RING + 1),
            scratch_shapes=[
                pltpu.VMEM((slots, plen, dslice), jnp.bfloat16),
                pltpu.VMEM((full + col_width, BLOCK), jnp.bfloat16),
                pltpu.SemaphoreType.DMA((slots,)),
                pltpu.SemaphoreType.DMA((2 * parts,)),
            ],
            compiler_params=params,
            cost_estimate=cost(n, n),
            name="forward",
        )(tab, *mine, w_blocks)

        sum_a = first_stage(partials[:RING], "x")
        sum_b = first_stage(partials[RING:], "y")
        terms_a = second_stage(sum_a, "y")
        terms_b = second_stage(sum_b, "x")
        tiles = half // TILE
        first = rank * 2 * tiles
        slope_a, pooled_a = activate(tile_table(table, first, tiles), terms_a)
        slope_b, pooled_b = activate(tile_table(table, first + tiles, tiles), terms_b)
        row_a = jnp.stack(spread(slope_a, "x"))
        column_b = jnp.stack(spread(slope_b, "y"))
        slopes = spread(row_a, "y") + spread(column_b, "x")

        def exchange(packed, table=table, cap=cap, rest=rest):
            height = rest // parts
            arrived = lax.all_to_all(
                packed.reshape(parts, height, BLOCK), "dp", split_axis=0, concat_axis=0, tiled=True
            )
            places = tile_table(table, cap // TILE + rank * (height // TILE), height // TILE)
            mine, pooled = activate(places, [arrived[i] for i in range(parts)])
            copies = jnp.broadcast_to(mine[None], (parts, height, BLOCK))
            spread_out = lax.all_to_all(copies, "dp", split_axis=0, concat_axis=0, tiled=True)
            return spread_out.reshape(rest, BLOCK), pooled

        near = [
            [min((j // 2 - k // 2) % CHIPS, (k // 2 - j // 2) % CHIPS) in rounds for k in range(batches)]
            for j in range(batches)
        ]
        most = jnp.max(jnp.sum(jnp.where(jnp.array(near), needed, 0), axis=0))
        slopes_over, pooled_over = lax.cond(
            most > cap,
            exchange,
            lambda packed: (
                jnp.zeros_like(packed),
                jnp.zeros((units, BLOCK), jnp.float32),
            ),
            over,
        )
        pooled_terms += [pooled_a, pooled_b, pooled_over]

        grads = pl.pallas_call(
            functools.partial(hidden_grad_kernel, cap, n),
            out_shape=[jax.ShapeDtypeStruct((OWN_SLOTS, plen, dslice), jnp.bfloat16)] * n,
            in_specs=[smem] + [any_spec] * (2 * RING + 1) + [vmem],
            out_specs=[any_spec] * n,
            scratch_shapes=[
                pltpu.VMEM((full + col_width, BLOCK), jnp.bfloat16),
                pltpu.VMEM((slots, plen, dslice), jnp.bfloat16),
                pltpu.SemaphoreType.DMA((2 * parts,)),
                pltpu.SemaphoreType.DMA((n,)),
            ],
            compiler_params=params,
            cost_estimate=cost(n, n),
            name="hidden_grad",
        )(tab, *slopes, slopes_over, w_blocks)
        for (step, same), value in sorted(zip(where, grads), key=lambda item: -abs(item[0][0])):
            back[(step, same)] = value if (step, same) == (0, True) else along(value, step, same)
        tabs.append(tab)
        slope_lists += slopes + [slopes_over]
        sizes.append((n, cap, full))
        all_held += mine

    pooled = sum(pooled_terms[1:], pooled_terms[0])
    pooled_parts = lax.all_to_all(
        pooled.reshape(parts, -1, BLOCK), "dp", split_axis=0, concat_axis=0, tiled=True
    )
    reps = jnp.sum(pooled_parts, axis=0).reshape(1, 1, OWN_SLOTS, col_width)

    moment_shape = jax.ShapeDtypeStruct((OWN_BLOCKS, BLOCK, dslice), jnp.bfloat16)
    packed_rows = sum(full for _, _, full in sizes)
    new_first, new_second = pl.pallas_call(
        functools.partial(weight_grad_kernel, tuple(sizes)),
        out_shape=(moment_shape, moment_shape),
        in_specs=[smem] * len(tabs) + [any_spec] * (batches + len(slope_lists)) + [vmem] * 2,
        out_specs=(vmem, vmem),
        scratch_shapes=[
            pltpu.VMEM((batches * OWN_SLOTS, plen, dslice), jnp.bfloat16),
            pltpu.VMEM((packed_rows + col_width, BLOCK), jnp.bfloat16),
            pltpu.VMEM((OWN_BLOCKS, BLOCK, dslice), jnp.float32),
            pltpu.SemaphoreType.DMA((batches * OWN_SLOTS,)),
            pltpu.SemaphoreType.DMA((len(tabs) * 2 * parts,)),
        ],
        compiler_params=params,
        cost_estimate=cost(batches, 24),
        name="weight_grad",
    )(
        *tabs,
        *all_held,
        *slope_lists,
        first_moment.reshape(moment_shape.shape),
        second_moment.reshape(moment_shape.shape),
    )

    arrived = positions(range(CHIPS // 2 + 1))
    owners = jnp.stack([device_at(chip, core, CHIPS - step, same) for step, same in arrived])
    grad_hidden = pl.pallas_call(
        gather_home_kernel,
        out_shape=jax.ShapeDtypeStruct(hidden.shape, jnp.bfloat16),
        in_specs=[smem] + [vmem] * batches,
        out_specs=vmem,
        scratch_shapes=[pltpu.VMEM(hidden.shape, jnp.float32)],
        compiler_params=params,
        cost_estimate=cost(1, 6),
        name="gather_home",
    )(reorder(home, owners).reshape(-1), *[back[key] for key in arrived])
    return (
        reps,
        grad_hidden,
        new_first.reshape(first_moment.shape),
        new_second.reshape(second_moment.shape),
    )


def solution(mesh):
    return jax.shard_map(
        shards,
        mesh=mesh,
        in_specs=(
            P("vocab", None, "dp"),
            P("vocab", "dp"),
            P("vocab"),
            P("vocab", "dp"),
            P("vocab", "dp"),
            P(None, "vocab", None),
            P(None, "vocab", None),
            P(),
            P(),
        ),
        out_specs=(
            P("dp", "vocab", None, None),
            P("vocab", None, "dp"),
            P("vocab", "dp"),
            P("vocab", "dp"),
        ),
        check_vma=False,
    )
```

```python
import functools

import jax
import jax.numpy as jnp
from jax import lax
from jax.experimental import pallas as pl
from jax.experimental.pallas import tpu as pltpu
from jax.sharding import PartitionSpec as P

BLOCK = 128
OWN_BLOCKS = 32
SLOT_BLOCKS = 4
OWN_SLOTS = 4
TILE = 16
RING = 4
CHIPS = 8
UNIT_ROWS = SLOT_BLOCKS * OWN_SLOTS * BLOCK
NEAR, FAR = (0, 1, 2), (3, 4)
CAP_SHARE, CAP_PARTS = 31, 64

beta_one = 0.9
beta_two = 0.999

PASS, COUNT, ROWS, OFF, LEN, IDS, GLOBAL, FIRST = 0, 1, 2, 3, 4, 5, 9, 10
WIDTH = 16
UNIT, START, TLEN, BIAS_ROW, COT_ROW = 0, 1, 2, 3, 4
TWIDTH = 8

CONTRACT_LAST = (((1,), (1,)), ((), ()))
CONTRACT_FIRST = (((0,), (0,)), ((), ()))
LIMIT = 60 * 1024 * 1024


def positions(rounds):
    out = []
    for r in rounds:
        if r == 0:
            out += [(0, True), (0, False)]
        elif 2 * r == CHIPS:
            out += [(r, True), (r, False)]
        else:
            out += [(-r, True), (r, True), (-r, False), (r, False)]
    return out


def device_at(chip, core, step, same):
    return lax.rem(chip + step + CHIPS, CHIPS) * 2 + (core if same else 1 - core)


def reorder(rows, order):
    pick = order[:, None] == jnp.arange(rows.shape[0], dtype=jnp.int32)[None, :]
    pick = pick.reshape(pick.shape + (1,) * (rows.ndim - 1))
    return jnp.sum(jnp.where(pick, rows[None], 0), axis=1)


def slot_columns(counts_all, ids, lengths, me):
    batches, per_batch, owners = counts_all.shape
    live = (counts_all > 0).astype(jnp.int32)
    place = jnp.arange(per_batch, dtype=jnp.int32)
    earlier = (place[None, :] < place[:, None]).astype(jnp.int32)
    rank = jnp.sum(live[:, None, :, :] * earlier[None, :, :, None], axis=2)
    slot_place = jnp.arange(OWN_SLOTS, dtype=jnp.int32)
    padded = (lengths + TILE - 1) // TILE * TILE
    needed = jnp.sum(counts_all * padded[:, :, None], axis=1)
    counts = lax.dynamic_index_in_dim(counts_all, me, 2, keepdims=False)
    live_me = lax.dynamic_index_in_dim(live, me, 2, keepdims=False)
    rank_me = lax.dynamic_index_in_dim(rank, me, 2, keepdims=False)
    chosen = (
        (live_me[:, None, :] == 1) & (rank_me[:, None, :] == slot_place[None, :, None])
    ).astype(jnp.int32)
    passage = jnp.sum(chosen * place[None, None, :], axis=2)
    count = jnp.sum(chosen * counts[:, None, :], axis=2)
    length = jnp.sum(chosen * lengths[:, None, :], axis=2)
    rows = jnp.sum(chosen * padded[:, None, :], axis=2)
    slot_ids = jnp.sum(chosen[:, :, :, None] * ids[:, None, :, :], axis=2)
    batch = jnp.arange(batches, dtype=jnp.int32)[:, None]
    base = jnp.stack(
        [passage, count, rows, jnp.zeros_like(rows), length]
        + [slot_ids[:, :, q] for q in range(SLOT_BLOCKS)]
        + [
            batch * per_batch + passage,
            (batch * OWN_SLOTS + slot_place[None, :]) * SLOT_BLOCKS,
        ],
        axis=2,
    )
    base = jnp.pad(base, ((0, 0), (0, 0), (0, WIDTH - base.shape[2])))
    live_home = lax.dynamic_index_in_dim(live, me, 0, keepdims=False)
    rank_home = lax.dynamic_index_in_dim(rank, me, 0, keepdims=False)
    at_home = (live_home[:, :, None] == 1) & (rank_home[:, :, None] == slot_place[None, None, :])
    home = jnp.sum(jnp.where(at_home, place[:, None, None] + 1, 0), axis=0) - 1
    return base, home, needed


def group_table(base, order):
    rows = reorder(base, order).reshape(-1, WIDTH)
    slots = rows.shape[0]
    line = jnp.arange(slots, dtype=jnp.int32)
    need = rows[:, COUNT] * rows[:, ROWS]
    off = jnp.sum(jnp.where(line[None, :] < line[:, None], need[None, :], 0), axis=1)
    column = jnp.arange(WIDTH, dtype=jnp.int32) == OFF
    return jnp.where(column[None, :], off[:, None], rows)


def tile_table(slots, first_tile, tiles):
    at = first_tile + jnp.arange(tiles, dtype=jnp.int32)
    starts = slots[:, OFF] // TILE
    holder = jnp.sum((starts[None, :] <= at[:, None]).astype(jnp.int32), axis=1) - 1
    mine = reorder(slots, holder)
    height = mine[:, ROWS] // TILE
    rel = at - mine[:, OFF] // TILE
    q = sum((rel >= height * n).astype(jnp.int32) for n in range(1, SLOT_BLOCKS))
    start = (rel - q * height) * TILE
    length = jnp.where(rel < height * mine[:, COUNT], mine[:, LEN], 0)
    which = jnp.arange(SLOT_BLOCKS, dtype=jnp.int32)
    block = jnp.sum(
        jnp.where(which[None, :] == q[:, None], mine[:, IDS : IDS + SLOT_BLOCKS], 0), axis=1
    )
    columns = [mine[:, FIRST] + q, start, length, block, mine[:, GLOBAL] * SLOT_BLOCKS + q]
    filler = jnp.zeros((tiles,), jnp.int32)
    return jnp.stack(columns + [filler] * (TWIDTH - len(columns)), axis=1).reshape(-1)


def slot_weights(w_ref, tab_ref, base):
    return jnp.concatenate([w_ref[tab_ref[base + IDS + q]] for q in range(SLOT_BLOCKS)], axis=0)


def slot_slopes(buf, tab_ref, base):
    count, rows = tab_ref[base + COUNT], tab_ref[base + ROWS]
    off, length = tab_ref[base + OFF], tab_ref[base + LEN]
    token = lax.broadcasted_iota(jnp.int32, (BLOCK, BLOCK), 0)
    pieces = []
    for q in range(SLOT_BLOCKS):
        at = pl.multiple_of(off + q * rows, TILE)
        value = buf[pl.ds(at, BLOCK), :]
        bound = jnp.where(q < count, length, 0)
        pieces.append(jnp.where(token < bound, value.astype(jnp.float32), 0.0).astype(jnp.bfloat16))
    return jnp.concatenate(pieces, axis=1)


def placed(tab_ref, slots, buf, pieces, sems, out):
    ahead, across = pieces[:RING], pieces[RING:]
    half = ahead[0].shape[1]
    x, y = tab_ref[slots * WIDTH], tab_ref[slots * WIDTH + 1]
    copies = []
    for dx in range(RING):
        for dy in range(RING):
            if out:
                to_x, to_y = x + dx, y + dy
                first, second = ahead[dx].at[dy], across[dy].at[dx]
            else:
                to_x, to_y = x - dx + RING, y - dy + RING
                first, second = ahead[dy].at[dx], across[dx].at[dy]
            owner = lax.rem(to_y, RING) * RING + lax.rem(to_x, RING)
            start = owner * (2 * half)
            for ref, at in ((first, start), (second, start + half)):
                view = buf.at[pl.ds(pl.multiple_of(at, TILE), half)]
                source, target = (view, ref) if out else (ref, view)
                copies.append(pltpu.make_async_copy(source, target, sems.at[len(copies)]))
    return copies


def packed_total(tab_ref, slots):
    base = (slots - 1) * WIDTH
    return tab_ref[base + OFF] + tab_ref[base + COUNT] * tab_ref[base + ROWS]


def fetch_passages(tab_ref, first, hidden_refs, hbuf, hsems):
    for i, ref in enumerate(hidden_refs):
        for s in range(OWN_SLOTS):
            at = i * OWN_SLOTS + s
            row = ref.at[tab_ref[(first + at) * WIDTH + PASS]]
            pltpu.make_async_copy(row, hbuf.at[at], hsems.at[at]).start()


def forward_slots(tab_ref, first, n, hidden_refs, w_ref, hbuf, buf, hsems):
    def step(t, carry):
        base = (first + t) * WIDTH
        rows, off = tab_ref[base + ROWS], tab_ref[base + OFF]
        pltpu.make_async_copy(hidden_refs[0].at[0], hbuf.at[t], hsems.at[t]).wait()

        @pl.when(tab_ref[base + COUNT] > 0)
        def _():
            value = lax.dot_general(
                hbuf[t],
                slot_weights(w_ref, tab_ref, base),
                CONTRACT_LAST,
                preferred_element_type=jnp.float32,
            ).astype(jnp.bfloat16)
            for q in range(SLOT_BLOCKS):
                at = pl.multiple_of(off + q * rows, TILE)
                buf[pl.ds(at, BLOCK), :] = value[:, q * BLOCK : (q + 1) * BLOCK]

        return carry

    lax.fori_loop(0, n * OWN_SLOTS, step, 0)


def forward_near_kernel(n, tab_ref, *refs):
    hidden_refs, w_ref = refs[:n], refs[n]
    out_ref, hbuf, buf, hsems, sem = refs[n + 1 :]
    fetch_passages(tab_ref, 0, hidden_refs, hbuf, hsems)
    forward_slots(tab_ref, 0, n, hidden_refs, w_ref, hbuf, buf, hsems)
    copy = pltpu.make_async_copy(buf.at[pl.ds(0, out_ref.shape[0])], out_ref, sem)
    copy.start()
    copy.wait()


def forward_far_kernel(cap, before, n, tab_ref, *refs):
    hidden_refs, w_ref, near_ref = refs[:n], refs[n], refs[n + 1]
    pieces = refs[n + 2 : n + 2 + 2 * RING]
    rest_ref, hbuf, buf, hsems, sems = refs[n + 2 + 2 * RING :]
    slots = (before + n) * OWN_SLOTS
    lower = near_ref.shape[0] // 2
    load = pltpu.make_async_copy(near_ref.at[pl.ds(0, lower)], buf.at[pl.ds(0, lower)], sems.at[0])
    load.start()
    fetch_passages(tab_ref, before * OWN_SLOTS, hidden_refs, hbuf, hsems)
    load.wait()

    @pl.when(packed_total(tab_ref, before * OWN_SLOTS) > lower)
    def _():
        more = pltpu.make_async_copy(
            near_ref.at[pl.ds(lower, lower)], buf.at[pl.ds(lower, lower)], sems.at[1]
        )
        more.start()
        more.wait()

    forward_slots(tab_ref, before * OWN_SLOTS, n, hidden_refs, w_ref, hbuf, buf, hsems)
    copies = placed(tab_ref, slots, buf, pieces, sems, True)
    for copy in copies:
        copy.start()
    for copy in copies:
        copy.wait()

    @pl.when(packed_total(tab_ref, slots) > cap)
    def _():
        more = pltpu.make_async_copy(buf.at[pl.ds(cap, rest_ref.shape[0])], rest_ref, sems.at[0])
        more.start()
        more.wait()


def activate_kernel(terms, tile_ref, bias_ref, cot_ref, *refs):
    pooled_ref = refs[-1]
    pooled_ref[...] = jnp.zeros_like(pooled_ref)
    taken, tile = 0, 0
    for g, count in enumerate(terms):
        slope_ref = refs[sum(terms) + g]
        lg_refs = refs[taken : taken + count]
        activate_block(tile, tile_ref, bias_ref, cot_ref, lg_refs, slope_ref, pooled_ref)
        taken, tile = taken + count, tile + slope_ref.shape[0] // TILE


def activate_block(tile, tile_ref, bias_ref, cot_ref, lg_refs, slope_ref, pooled_ref):
    def step(i, carry):
        base = (tile + i) * TWIDTH
        unit, start = tile_ref[base + UNIT], tile_ref[base + START]
        length, bias_row = tile_ref[base + TLEN], tile_ref[base + BIAS_ROW]
        cot_row = tile_ref[base + COT_ROW]
        at = pl.multiple_of(i * TILE, TILE)
        x = bias_ref[pl.ds(bias_row, 1), :]
        for lg_ref in lg_refs:
            x = x + lg_ref[pl.ds(at, TILE), :].astype(jnp.float32)
        token = lax.broadcasted_iota(jnp.int32, x.shape, 0) + start
        keep = token < length
        divisor = jnp.full((1, BLOCK), jnp.maximum(length, 1), jnp.int32).astype(jnp.float32)
        weight = 1.0 / divisor
        small = jnp.exp(-jnp.abs(x))
        soft = jnp.maximum(x, 0.0) + jnp.log1p(small)
        sig = jnp.where(x >= 0, 1.0, small) / (1.0 + small)
        gain = jnp.where(keep, jnp.log1p(soft) * weight, 0.0)
        pooled_ref[pl.ds(unit, 1), :] += jnp.sum(gain, axis=0, keepdims=True)
        cot = cot_ref[pl.ds(cot_row, 1), :] * weight
        slope = jnp.where(keep, cot * sig / (1.0 + soft), 0.0)
        slope_ref[pl.ds(at, TILE), :] = slope.astype(jnp.bfloat16)
        return carry

    lax.fori_loop(0, slope_ref.shape[0] // TILE, step, 0)


def load_slopes(cap, tab_ref, pieces, rest_ref, buf, sems, slots):
    copies = placed(tab_ref, slots, buf, pieces, sems, False)
    for copy in copies:
        copy.start()
    for copy in copies:
        copy.wait()

    @pl.when(packed_total(tab_ref, slots) > cap)
    def _():
        more = pltpu.make_async_copy(rest_ref, buf.at[pl.ds(cap, rest_ref.shape[0])], sems.at[0])
        more.start()
        more.wait()


def hidden_grad_kernel(cap, all_slots, first, n, tab_ref, *refs):
    pieces = refs[: 2 * RING]
    rest_ref, w_ref = refs[2 * RING : 2 * RING + 2]
    out_refs = refs[2 * RING + 2 : 2 * RING + 2 + n]
    buf, obuf, sems, osems = refs[2 * RING + 2 + n :]
    load_slopes(cap, tab_ref, pieces, rest_ref, buf, sems, all_slots)

    def step(t, carry):
        base = (first + t) * WIDTH
        live = tab_ref[base + COUNT] > 0

        @pl.when(live)
        def _():
            value = jnp.dot(
                slot_slopes(buf, tab_ref, base),
                slot_weights(w_ref, tab_ref, base),
                preferred_element_type=jnp.float32,
            )
            obuf[t] = value.astype(jnp.bfloat16)

        @pl.when(jnp.logical_not(live))
        def _():
            obuf[t] = jnp.zeros(obuf.shape[1:], jnp.bfloat16)

        return carry

    lax.fori_loop(0, n * OWN_SLOTS, step, 0)
    done = [
        pltpu.make_async_copy(obuf.at[pl.ds(i * OWN_SLOTS, OWN_SLOTS)], out_refs[i], osems.at[i])
        for i in range(n)
    ]
    for copy in done:
        copy.start()
    for copy in done:
        copy.wait()


def weight_grad_kernel(cap, n, tab_ref, *refs):
    hidden_refs, pieces = refs[:n], refs[n : n + 2 * RING]
    rest_ref, m_ref, v_ref, first_ref, second_ref = refs[n + 2 * RING : n + 2 * RING + 5]
    hbuf, buf, acc, hsems, sems = refs[n + 2 * RING + 5 :]
    slots = n * OWN_SLOTS
    fetch_passages(tab_ref, 0, hidden_refs, hbuf, hsems)
    acc[...] = jnp.zeros_like(acc)
    load_slopes(cap, tab_ref, pieces, rest_ref, buf, sems, slots)

    def step(t, carry):
        base = t * WIDTH
        pltpu.make_async_copy(hidden_refs[0].at[0], hbuf.at[t], hsems.at[t]).wait()

        @pl.when(tab_ref[base + COUNT] > 0)
        def _():
            value = lax.dot_general(
                slot_slopes(buf, tab_ref, base),
                hbuf[t],
                CONTRACT_FIRST,
                preferred_element_type=jnp.float32,
            )
            for q in range(SLOT_BLOCKS):
                acc[tab_ref[base + IDS + q]] += value[q * BLOCK : (q + 1) * BLOCK]

        return carry

    lax.fori_loop(0, slots, step, 0)

    def update(i, carry):
        grad = acc[i]
        m, v = m_ref[i].astype(jnp.float32), v_ref[i].astype(jnp.float32)
        first_ref[i] = (beta_one * m + (1.0 - beta_one) * grad).astype(jnp.bfloat16)
        second_ref[i] = (beta_two * v + (1.0 - beta_two) * grad * grad).astype(jnp.bfloat16)
        return carry

    lax.fori_loop(0, acc.shape[0], update, 0)


def gather_home_kernel(home_ref, *refs):
    terms, out_ref, acc = refs[:-2], refs[-2], refs[-1]
    acc[...] = jnp.zeros_like(acc)
    for i, term in enumerate(terms):
        for s in range(OWN_SLOTS):
            local = home_ref[i * OWN_SLOTS + s]

            @pl.when(local >= 0)
            def _():
                acc[local] += term[s].astype(jnp.float32)

    out_ref[...] = acc[...].astype(jnp.bfloat16)


def shards(
    hidden,
    weights,
    bias,
    first_moment,
    second_moment,
    rep_cot,
    active_blocks,
    block_counts,
    passage_len,
):
    batches = lax.axis_size("vocab")
    parts = lax.axis_size("dp")
    per_batch, plen, dslice = hidden.shape
    col_width = SLOT_BLOCKS * BLOCK
    me = lax.axis_index("vocab")
    chip, core = me // 2, lax.rem(me, 2)
    rank = lax.axis_index("dp")

    def along(value, step, same=True):
        pairs = []
        for z in range(CHIPS):
            for c in range(2):
                pairs.append((2 * z + c, 2 * ((z + step) % CHIPS) + (c if same else 1 - c)))
        return lax.ppermute(value, "vocab", pairs)

    held = {(0, True): hidden, (0, False): along(hidden, 0, False)}
    up = down = hidden
    for r in range(1, CHIPS // 2):
        up, down = along(up, 1), along(down, -1)
        held[(-r, True)], held[(r, True)] = up, down
        held[(-r, False)], held[(r, False)] = along(up, 0, False), along(down, 0, False)
    far = jnp.where(core == 0, up, down)
    pairs = []
    for z in range(CHIPS):
        pairs += [(2 * z, 2 * ((z + 1) % CHIPS)), (2 * z + 1, 2 * ((z - 1) % CHIPS) + 1)]
    far = lax.ppermute(far, "vocab", pairs)
    held[(CHIPS // 2, True)] = far
    held[(CHIPS // 2, False)] = along(far, 0, False)

    base, home, needed = slot_columns(
        block_counts.reshape(batches, per_batch, batches),
        active_blocks.reshape(batches, per_batch, SLOT_BLOCKS),
        passage_len.reshape(batches, per_batch),
        me,
    )
    line = jnp.arange(WIDTH)
    corner = jnp.where(line == 0, lax.rem(rank, RING), jnp.where(line == 1, rank // RING, 0))
    corner = corner.astype(jnp.int32)
    cot_rows = rep_cot.astype(jnp.float32).reshape(-1, BLOCK)
    bias_rows = bias.reshape(OWN_BLOCKS, BLOCK)
    w_blocks = weights.reshape(OWN_BLOCKS, BLOCK, dslice)
    units = batches * OWN_SLOTS * SLOT_BLOCKS

    any_spec = pl.BlockSpec(memory_space=pl.ANY)
    vmem = pl.BlockSpec(memory_space=pltpu.VMEM)
    smem = pl.BlockSpec(memory_space=pltpu.SMEM)
    params = pltpu.CompilerParams(vmem_limit_bytes=LIMIT)

    def cost(n, count):
        flops = 2 * n * UNIT_ROWS * BLOCK * dslice // BLOCK
        return pl.CostEstimate(flops=flops, bytes_accessed=count * 1024 * 1024, transcendentals=0)

    def activate(places, blocks):
        heights = [terms[0].shape[0] for terms in blocks]
        counts = tuple(len(terms) for terms in blocks)
        return pl.pallas_call(
            functools.partial(activate_kernel, counts),
            out_shape=(
                *[jax.ShapeDtypeStruct((height, BLOCK), jnp.bfloat16) for height in heights],
                jax.ShapeDtypeStruct((units, BLOCK), jnp.float32),
            ),
            in_specs=[smem] + [vmem] * (2 + sum(counts)),
            out_specs=(vmem,) * (len(blocks) + 1),
            name="activate",
        )(places, bias_rows, cot_rows, *[term for terms in blocks for term in terms])

    def move(value, axis, step):
        pairs = []
        for y in range(RING):
            for x in range(RING):
                to_x, to_y = ((x + step) % RING, y) if axis == "x" else (x, (y + step) % RING)
                pairs.append((y * RING + x, to_y * RING + to_x))
        return lax.ppermute(value, "dp", pairs)

    steps = (1, 3, 2)

    def first_stage(terms, axis):
        arrived = [move(terms[d], axis, d) for d in steps]
        total = terms[0].astype(jnp.float32)
        for value in arrived:
            total = total + value.astype(jnp.float32)
        return total.astype(jnp.bfloat16)

    def second_stage(summed, axis):
        return [summed[0]] + [move(summed[d], axis, d) for d in steps]

    def spread(value, axis):
        arrived = {d: move(value, axis, d) for d in steps}
        return [value] + [arrived[d] for d in range(1, RING)]

    near, far_off = positions(NEAR), positions(FAR)
    where = near + far_off
    slots = batches * OWN_SLOTS
    full = batches * UNIT_ROWS
    cap = full * CAP_SHARE // CAP_PARTS
    rest, half = full - cap, cap // parts // 2
    order = jnp.stack([device_at(chip, core, step, same) for step, same in where])
    table = group_table(base, order)
    tab = jnp.concatenate([table.reshape(-1), corner])
    piece = jax.ShapeDtypeStruct((RING, half, BLOCK), jnp.bfloat16)
    near_rows = len(near) * UNIT_ROWS
    buf_shape = pltpu.VMEM((full + col_width, BLOCK), jnp.bfloat16)
    piece_sems = pltpu.SemaphoreType.DMA((2 * parts,))

    def passages(n):
        return pltpu.VMEM((n * OWN_SLOTS, plen, dslice), jnp.bfloat16)

    def passage_sems(n):
        return pltpu.SemaphoreType.DMA((n * OWN_SLOTS,))

    near_packed = pl.pallas_call(
        functools.partial(forward_near_kernel, len(near)),
        out_shape=jax.ShapeDtypeStruct((near_rows, BLOCK), jnp.bfloat16),
        in_specs=[smem] + [any_spec] * len(near) + [vmem],
        out_specs=any_spec,
        scratch_shapes=[
            passages(len(near)),
            pltpu.VMEM((near_rows + col_width, BLOCK), jnp.bfloat16),
            passage_sems(len(near)),
            pltpu.SemaphoreType.DMA,
        ],
        compiler_params=params,
        cost_estimate=cost(len(near), len(near)),
        name="forward_near",
    )(tab, *[held[key] for key in near], w_blocks)
    *partials, over = pl.pallas_call(
        functools.partial(forward_far_kernel, cap, len(near), len(far_off)),
        out_shape=(*[piece] * (2 * RING), jax.ShapeDtypeStruct((rest, BLOCK), jnp.bfloat16)),
        in_specs=[smem] + [any_spec] * len(far_off) + [vmem, any_spec],
        out_specs=(any_spec,) * (2 * RING + 1),
        scratch_shapes=[passages(len(far_off)), buf_shape, passage_sems(len(far_off)), piece_sems],
        compiler_params=params,
        cost_estimate=cost(len(far_off), 10),
        name="forward_far",
    )(tab, *[held[key] for key in far_off], w_blocks, near_packed)

    sum_a = first_stage(partials[:RING], "x")
    sum_b = first_stage(partials[RING:], "y")
    terms_a = second_stage(sum_a, "y")
    terms_b = second_stage(sum_b, "x")
    tiles = 2 * half // TILE
    slope_a, slope_b, pooled = activate(
        tile_table(table, rank * tiles, tiles), [terms_a, terms_b]
    )
    row_a = jnp.stack(spread(slope_a, "x"))
    column_b = jnp.stack(spread(slope_b, "y"))
    slopes = spread(row_a, "y") + spread(column_b, "x")

    def exchange(packed):
        height = rest // parts
        arrived = lax.all_to_all(
            packed.reshape(parts, height, BLOCK), "dp", split_axis=0, concat_axis=0, tiled=True
        )
        places = tile_table(table, cap // TILE + rank * (height // TILE), height // TILE)
        mine, pooled_mine = activate(places, [[arrived[i] for i in range(parts)]])
        copies = jnp.broadcast_to(mine[None], (parts, height, BLOCK))
        spread_out = lax.all_to_all(copies, "dp", split_axis=0, concat_axis=0, tiled=True)
        return spread_out.reshape(rest, BLOCK), pooled_mine

    most = jnp.max(jnp.sum(needed, axis=0))
    slopes_over, pooled_over = lax.cond(
        most > cap,
        exchange,
        lambda packed: (jnp.zeros_like(packed), jnp.zeros((units, BLOCK), jnp.float32)),
        over,
    )

    back = {}
    for first, group in ((len(near) * OWN_SLOTS, far_off), (0, near)):
        n = len(group)
        grads = pl.pallas_call(
            functools.partial(hidden_grad_kernel, cap, slots, first, n),
            out_shape=[jax.ShapeDtypeStruct((OWN_SLOTS, plen, dslice), jnp.bfloat16)] * n,
            in_specs=[smem] + [any_spec] * (2 * RING + 1) + [vmem],
            out_specs=[any_spec] * n,
            scratch_shapes=[buf_shape, passages(n), piece_sems, pltpu.SemaphoreType.DMA((n,))],
            compiler_params=params,
            cost_estimate=cost(n, n),
            name="hidden_grad",
        )(tab, *slopes, slopes_over, w_blocks)
        for (step, same), value in sorted(zip(group, grads), key=lambda item: -abs(item[0][0])):
            back[(step, same)] = value if (step, same) == (0, True) else along(value, step, same)

    pooled_parts = lax.all_to_all(
        (pooled + pooled_over).reshape(parts, -1, BLOCK),
        "dp",
        split_axis=0,
        concat_axis=0,
        tiled=True,
    )
    reps = jnp.sum(pooled_parts, axis=0).reshape(1, 1, OWN_SLOTS, col_width)

    moment_shape = jax.ShapeDtypeStruct((OWN_BLOCKS, BLOCK, dslice), jnp.bfloat16)
    new_first, new_second = pl.pallas_call(
        functools.partial(weight_grad_kernel, cap, batches),
        out_shape=(moment_shape, moment_shape),
        in_specs=[smem] + [any_spec] * (batches + 2 * RING + 1) + [vmem] * 2,
        out_specs=(vmem, vmem),
        scratch_shapes=[
            passages(batches),
            buf_shape,
            pltpu.VMEM((OWN_BLOCKS, BLOCK, dslice), jnp.float32),
            passage_sems(batches),
            piece_sems,
        ],
        compiler_params=params,
        cost_estimate=cost(batches, 24),
        name="weight_grad",
    )(
        tab,
        *[held[key] for key in where],
        *slopes,
        slopes_over,
        first_moment.reshape(moment_shape.shape),
        second_moment.reshape(moment_shape.shape),
    )

    arrived = positions(range(CHIPS // 2 + 1))
    owners = jnp.stack([device_at(chip, core, CHIPS - step, same) for step, same in arrived])
    grad_hidden = pl.pallas_call(
        gather_home_kernel,
        out_shape=jax.ShapeDtypeStruct(hidden.shape, jnp.bfloat16),
        in_specs=[smem] + [vmem] * batches,
        out_specs=vmem,
        scratch_shapes=[pltpu.VMEM(hidden.shape, jnp.float32)],
        compiler_params=params,
        cost_estimate=cost(1, 6),
        name="gather_home",
    )(reorder(home, owners).reshape(-1), *[back[key] for key in arrived])
    return (
        reps,
        grad_hidden,
        new_first.reshape(first_moment.shape),
        new_second.reshape(second_moment.shape),
    )


def solution(mesh):
    return jax.shard_map(
        shards,
        mesh=mesh,
        in_specs=(
            P("vocab", None, "dp"),
            P("vocab", "dp"),
            P("vocab"),
            P("vocab", "dp"),
            P("vocab", "dp"),
            P(None, "vocab", None),
            P(None, "vocab", None),
            P(),
            P(),
        ),
        out_specs=(
            P("dp", "vocab", None, None),
            P("vocab", None, "dp"),
            P("vocab", "dp"),
            P("vocab", "dp"),
        ),
        check_vma=False,
    )
```

```python
import functools

import jax
import jax.numpy as jnp
from jax import lax
from jax.experimental import pallas as pl
from jax.experimental.pallas import tpu as pltpu
from jax.sharding import PartitionSpec as P

BLOCK = 128
OWN_BLOCKS = 32
SLOT_BLOCKS = 4
OWN_SLOTS = 4
TILE = 16
RING = 4
CAP_SHARE = 15
CAP_PARTS = 32

beta_one = 0.9
beta_two = 0.999

PASS, COUNT, ROWS, OFF, LEN, IDS = 0, 1, 2, 3, 4, 5
WIDTH = 16
UNIT, START, TLEN, BIAS_ROW, COT_ROW = 0, 1, 2, 3, 4
TWIDTH = 8

CONTRACT_LAST = (((1,), (1,)), ((), ()))
CONTRACT_FIRST = (((0,), (0,)), ((), ()))


def slot_table(counts_all, ids, lengths, me):
    batches, per_batch, owners = counts_all.shape
    live = (counts_all > 0).astype(jnp.int32)
    place = jnp.arange(per_batch, dtype=jnp.int32)
    earlier = (place[None, :] < place[:, None]).astype(jnp.int32)
    rank = jnp.sum(live[:, None, :, :] * earlier[None, :, :, None], axis=2)
    slot_place = jnp.arange(OWN_SLOTS, dtype=jnp.int32)
    padded = (lengths + TILE - 1) // TILE * TILE
    kept = live * (rank < OWN_SLOTS)
    totals = jnp.sum(kept * counts_all * padded[:, :, None], axis=(0, 1))
    counts = lax.dynamic_index_in_dim(counts_all, me, 2, keepdims=False)
    live_me = lax.dynamic_index_in_dim(live, me, 2, keepdims=False)
    rank_me = lax.dynamic_index_in_dim(rank, me, 2, keepdims=False)
    chosen = (
        (live_me[:, None, :] == 1) & (rank_me[:, None, :] == slot_place[None, :, None])
    ).astype(jnp.int32)
    first = jnp.arange(batches, dtype=jnp.int32)[:, None] * per_batch
    passage = jnp.sum(chosen * place[None, None, :], axis=2) + first
    count = jnp.sum(chosen * counts[:, None, :], axis=2)
    length = jnp.sum(chosen * lengths[:, None, :], axis=2)
    rows = jnp.sum(chosen * padded[:, None, :], axis=2)
    slot_ids = jnp.sum(chosen[:, :, :, None] * ids[:, None, :, :], axis=2)
    slots = batches * OWN_SLOTS
    need = (count * rows).reshape(slots)
    order = jnp.arange(slots, dtype=jnp.int32)
    off = jnp.sum(jnp.where(order[None, :] < order[:, None], need[None, :], 0), axis=1)
    columns = [
        passage.reshape(slots, 1),
        count.reshape(slots, 1),
        rows.reshape(slots, 1),
        off.reshape(slots, 1),
        length.reshape(slots, 1),
        slot_ids.reshape(slots, SLOT_BLOCKS),
        jnp.zeros((slots, WIDTH - IDS - SLOT_BLOCKS), jnp.int32),
    ]
    return jnp.concatenate(columns, axis=1), jnp.max(totals)


def tile_table(slots, first_tile, tiles):
    at = first_tile + jnp.arange(tiles, dtype=jnp.int32)
    starts = slots[:, OFF] // TILE
    holder = jnp.sum((starts[None, :] <= at[:, None]).astype(jnp.int32), axis=1) - 1
    order = jnp.arange(slots.shape[0], dtype=jnp.int32)
    pick = (holder[:, None] == order[None, :]).astype(jnp.int32)
    mine = jnp.sum(pick[:, :, None] * slots[None, :, :], axis=1)
    height = mine[:, ROWS] // TILE
    rel = at - mine[:, OFF] // TILE
    q = sum((rel >= height * n).astype(jnp.int32) for n in range(1, SLOT_BLOCKS))
    start = (rel - q * height) * TILE
    length = jnp.where(rel < height * mine[:, COUNT], mine[:, LEN], 0)
    which = jnp.arange(SLOT_BLOCKS, dtype=jnp.int32)
    block = jnp.sum(
        jnp.where(which[None, :] == q[:, None], mine[:, IDS : IDS + SLOT_BLOCKS], 0), axis=1
    )
    columns = [
        holder * SLOT_BLOCKS + q,
        start,
        length,
        block,
        mine[:, PASS] * SLOT_BLOCKS + q,
    ]
    filler = jnp.zeros((tiles,), jnp.int32)
    return jnp.stack(columns + [filler] * (TWIDTH - len(columns)), axis=1).reshape(-1)


def slot_weights(w_ref, tab_ref, base):
    return jnp.concatenate([w_ref[tab_ref[base + IDS + q]] for q in range(SLOT_BLOCKS)], axis=0)


def slot_slopes(buf, tab_ref, base):
    plen = BLOCK
    count, rows = tab_ref[base + COUNT], tab_ref[base + ROWS]
    off, length = tab_ref[base + OFF], tab_ref[base + LEN]
    token = lax.broadcasted_iota(jnp.int32, (plen, BLOCK), 0)
    pieces = []
    for q in range(SLOT_BLOCKS):
        at = pl.multiple_of(off + q * rows, TILE)
        value = buf[pl.ds(at, plen), :]
        bound = jnp.where(q < count, length, 0)
        pieces.append(jnp.where(token < bound, value.astype(jnp.float32), 0.0).astype(jnp.bfloat16))
    return jnp.concatenate(pieces, axis=1)


def placed(tab_ref, slots, buf, pieces, sems, out):
    ahead, across = pieces[:RING], pieces[RING:]
    half = ahead[0].shape[1]
    base = slots * WIDTH
    x, y = tab_ref[base], tab_ref[base + 1]
    copies = []
    for dx in range(RING):
        for dy in range(RING):
            if out:
                to_x, to_y = x + dx, y + dy
            else:
                to_x, to_y = x - dx + RING, y - dy + RING
            owner = lax.rem(to_y, RING) * RING + lax.rem(to_x, RING)
            start = pl.multiple_of(owner * (2 * half), TILE)
            if out:
                first, second = ahead[dx].at[dy], across[dy].at[dx]
            else:
                first, second = ahead[dy].at[dx], across[dx].at[dy]
            for ref, at in ((first, start), (second, pl.multiple_of(start + half, TILE))):
                view = buf.at[pl.ds(at, half)]
                source, target = (view, ref) if out else (ref, view)
                copies.append(pltpu.make_async_copy(source, target, sems.at[len(copies)]))
    return copies


def packed_total(tab_ref, slots):
    base = (slots - 1) * WIDTH
    return tab_ref[base + OFF] + tab_ref[base + COUNT] * tab_ref[base + ROWS]


def forward_kernel(cap, tab_ref, *refs):
    hidden_refs, w_ref = refs[:OWN_SLOTS], refs[OWN_SLOTS]
    pieces = refs[OWN_SLOTS + 1 : OWN_SLOTS + 1 + 2 * RING]
    rest_ref, buf, sems = refs[OWN_SLOTS + 1 + 2 * RING :]
    j = pl.program_id(0)
    slots = pl.num_programs(0) * OWN_SLOTS
    for s in range(OWN_SLOTS):
        base = (j * OWN_SLOTS + s) * WIDTH
        count, rows, off = tab_ref[base + COUNT], tab_ref[base + ROWS], tab_ref[base + OFF]

        @pl.when(count > 0)
        def _():
            value = lax.dot_general(
                hidden_refs[s][0],
                slot_weights(w_ref, tab_ref, base),
                CONTRACT_LAST,
                preferred_element_type=jnp.float32,
            ).astype(jnp.bfloat16)
            for q in range(SLOT_BLOCKS):
                at = pl.multiple_of(off + q * rows, TILE)
                buf[pl.ds(at, BLOCK), :] = value[:, q * BLOCK : (q + 1) * BLOCK]

    @pl.when(j == pl.num_programs(0) - 1)
    def _():
        copies = placed(tab_ref, slots, buf, pieces, sems, True)
        for copy in copies:
            copy.start()
        for copy in copies:
            copy.wait()

        @pl.when(packed_total(tab_ref, slots) > cap)
        def _():
            more = pltpu.make_async_copy(
                buf.at[pl.ds(cap, rest_ref.shape[0])], rest_ref, sems.at[0]
            )
            more.start()
            more.wait()


def activate_kernel(tiles, tile_ref, bias_ref, cot_ref, *refs):
    lg_refs, (slope_ref, pooled_ref) = refs[:-2], refs[-2:]
    pooled_ref[...] = jnp.zeros_like(pooled_ref)

    def step(i, carry):
        base = i * TWIDTH
        unit, start = tile_ref[base + UNIT], tile_ref[base + START]
        length, bias_row = tile_ref[base + TLEN], tile_ref[base + BIAS_ROW]
        cot_row = tile_ref[base + COT_ROW]
        at = pl.multiple_of(i * TILE, TILE)
        x = bias_ref[pl.ds(bias_row, 1), :]
        for lg_ref in lg_refs:
            x = x + lg_ref[pl.ds(at, TILE), :].astype(jnp.float32)
        token = lax.broadcasted_iota(jnp.int32, x.shape, 0) + start
        keep = token < length
        divisor = jnp.full((1, BLOCK), jnp.maximum(length, 1), jnp.int32).astype(jnp.float32)
        weight = 1.0 / divisor
        small = jnp.exp(-jnp.abs(x))
        soft = jnp.maximum(x, 0.0) + jnp.log1p(small)
        sig = jnp.where(x >= 0, 1.0, small) / (1.0 + small)
        gain = jnp.where(keep, jnp.log1p(soft) * weight, 0.0)
        pooled_ref[pl.ds(unit, 1), :] += jnp.sum(gain, axis=0, keepdims=True)
        cot = cot_ref[pl.ds(cot_row, 1), :] * weight
        slope = jnp.where(keep, cot * sig / (1.0 + soft), 0.0)
        slope_ref[pl.ds(at, TILE), :] = slope.astype(jnp.bfloat16)
        return carry

    lax.fori_loop(0, tiles, step, 0, unroll=4)


def collect_kernel(*refs):
    terms, outs, sems = refs[: 2 * RING], refs[2 * RING : 2 * RING + 2], refs[-1]
    copies = []
    for i, term in enumerate(terms):
        target = outs[i // RING].at[i % RING]
        copies.append(pltpu.make_async_copy(term, target, sems.at[i]))
    for copy in copies:
        copy.start()
    for copy in copies:
        copy.wait()


def load_slopes(cap, tab_ref, pieces, rest_ref, buf, sems, slots):
    copies = placed(tab_ref, slots, buf, pieces, sems, False)
    for copy in copies:
        copy.start()
    for copy in copies:
        copy.wait()

    @pl.when(packed_total(tab_ref, slots) > cap)
    def _():
        more = pltpu.make_async_copy(rest_ref, buf.at[pl.ds(cap, rest_ref.shape[0])], sems.at[0])
        more.start()
        more.wait()


def hidden_grad_kernel(cap, tab_ref, *refs):
    pieces = refs[: 2 * RING]
    rest_ref, w_ref, out_ref, buf, sems = refs[2 * RING :]
    j = pl.program_id(0)

    @pl.when(j == 0)
    def _():
        load_slopes(cap, tab_ref, pieces, rest_ref, buf, sems, pl.num_programs(0) * OWN_SLOTS)

    out_ref[...] = jnp.zeros_like(out_ref)
    per_batch = out_ref.shape[0]
    for s in range(OWN_SLOTS):
        base = (j * OWN_SLOTS + s) * WIDTH
        local = tab_ref[base + PASS] - j * per_batch

        @pl.when(tab_ref[base + COUNT] > 0)
        def _():
            value = jnp.dot(
                slot_slopes(buf, tab_ref, base),
                slot_weights(w_ref, tab_ref, base),
                preferred_element_type=jnp.float32,
            )
            out_ref[local] = value.astype(jnp.bfloat16)


def weight_grad_kernel(cap, batches, tab_ref, *refs):
    hidden_refs, pieces = refs[:OWN_SLOTS], refs[OWN_SLOTS : OWN_SLOTS + 2 * RING]
    rest_ref, m_ref, v_ref, first_ref, second_ref, buf, acc, sems = refs[OWN_SLOTS + 2 * RING :]
    i = pl.program_id(0)

    @pl.when(i == 0)
    def _():
        load_slopes(cap, tab_ref, pieces, rest_ref, buf, sems, batches * OWN_SLOTS)
        acc[...] = jnp.zeros_like(acc)

    @pl.when(i < batches)
    def _():
        for s in range(OWN_SLOTS):
            base = (i * OWN_SLOTS + s) * WIDTH

            @pl.when(tab_ref[base + COUNT] > 0)
            def _():
                value = lax.dot_general(
                    slot_slopes(buf, tab_ref, base),
                    hidden_refs[s][0],
                    CONTRACT_FIRST,
                    preferred_element_type=jnp.float32,
                )
                for q in range(SLOT_BLOCKS):
                    acc[tab_ref[base + IDS + q]] += value[q * BLOCK : (q + 1) * BLOCK]

    @pl.when(i >= batches)
    def _():
        group = m_ref.shape[0]
        at = (i - batches) * group
        grad = acc[pl.ds(at, group)]
        m = m_ref[...].astype(jnp.float32)
        v = v_ref[...].astype(jnp.float32)
        first_ref[...] = (beta_one * m + (1.0 - beta_one) * grad).astype(jnp.bfloat16)
        second_ref[...] = (beta_two * v + (1.0 - beta_two) * grad * grad).astype(jnp.bfloat16)


def shards(
    hidden,
    weights,
    bias,
    first_moment,
    second_moment,
    rep_cot,
    active_blocks,
    block_counts,
    passage_len,
):
    batches = lax.axis_size("vocab")
    parts = lax.axis_size("dp")
    per_batch, plen, dslice = hidden.shape
    col_width = SLOT_BLOCKS * BLOCK
    slots = batches * OWN_SLOTS
    full = slots * SLOT_BLOCKS * plen
    cap = full * CAP_SHARE // CAP_PARTS
    rest = full - cap
    slack = 2 * BLOCK
    me = lax.axis_index("vocab")
    rank = lax.axis_index("dp")

    rows_all = lax.all_gather(hidden, "vocab", axis=0, tiled=True)

    table, most = slot_table(
        block_counts.reshape(batches, per_batch, batches),
        active_blocks.reshape(batches, per_batch, SLOT_BLOCKS),
        passage_len.reshape(batches, per_batch),
        me,
    )
    place = jnp.where(
        jnp.arange(WIDTH) == 0, lax.rem(rank, RING), jnp.where(jnp.arange(WIDTH) == 1, rank // RING, 0)
    )
    tab = jnp.concatenate([table.reshape(-1), place.astype(jnp.int32)])
    cot_rows = rep_cot.astype(jnp.float32).reshape(-1, BLOCK)
    bias_rows = bias.reshape(OWN_BLOCKS, BLOCK)
    w_blocks = weights.reshape(OWN_BLOCKS, BLOCK, dslice)

    any_spec = pl.BlockSpec(memory_space=pl.ANY)
    vmem = pl.BlockSpec(memory_space=pltpu.VMEM)
    smem = pl.BlockSpec(memory_space=pltpu.SMEM)

    def passage_spec(s):
        def index(i, t):
            row = jnp.minimum(i, batches - 1) * OWN_SLOTS + s
            return (t[row * WIDTH + PASS], 0, 0)

        return pl.BlockSpec((1, plen, dslice), index)

    passage_specs = [passage_spec(s) for s in range(OWN_SLOTS)]
    w_spec = pl.BlockSpec(
        w_blocks.shape, lambda i, t: (0, 0, 0), pipeline_mode=pl.Buffered(buffer_count=1)
    )
    buf_shape = pltpu.VMEM((full + slack, BLOCK), jnp.bfloat16)
    sems = pltpu.SemaphoreType.DMA((2 * parts,))
    half = cap // parts // 2
    piece = jax.ShapeDtypeStruct((RING, half, BLOCK), jnp.bfloat16)
    limit = 60 * 1024 * 1024
    flops = 2 * slots * plen * col_width * dslice

    *partials, over = pl.pallas_call(
        functools.partial(forward_kernel, cap),
        out_shape=(*[piece] * (2 * RING), jax.ShapeDtypeStruct((rest, BLOCK), jnp.bfloat16)),
        grid_spec=pltpu.PrefetchScalarGridSpec(
            num_scalar_prefetch=1,
            grid=(batches,),
            in_specs=passage_specs + [w_spec],
            out_specs=(any_spec,) * (2 * RING + 1),
            scratch_shapes=[buf_shape, sems],
        ),
        compiler_params=pltpu.CompilerParams(vmem_limit_bytes=limit),
        cost_estimate=pl.CostEstimate(
            flops=flops, bytes_accessed=16 * 1024 * 1024, transcendentals=0
        ),
        name="forward",
    )(tab, *([rows_all] * OWN_SLOTS), w_blocks)

    def activate(places, terms):
        height = terms[0].shape[0]
        return pl.pallas_call(
            functools.partial(activate_kernel, height // TILE),
            out_shape=(
                jax.ShapeDtypeStruct((height, BLOCK), jnp.bfloat16),
                jax.ShapeDtypeStruct((slots * SLOT_BLOCKS, BLOCK), jnp.float32),
            ),
            in_specs=[smem] + [vmem] * (2 + len(terms)),
            out_specs=(vmem, vmem),
            name="activate",
        )(places, bias_rows, cot_rows, *terms)

    def move(value, axis, step):
        pairs = []
        for y in range(RING):
            for x in range(RING):
                to_x, to_y = ((x + step) % RING, y) if axis == "x" else (x, (y + step) % RING)
                pairs.append((y * RING + x, to_y * RING + to_x))
        return lax.ppermute(value, "dp", pairs)

    steps = (1, 3, 2)

    def first_stage(terms, axis):
        arrived = [move(terms[d], axis, d) for d in steps]
        total = terms[0].astype(jnp.float32)
        for value in arrived:
            total = total + value.astype(jnp.float32)
        return total.astype(jnp.bfloat16)

    def second_stage(summed, axis):
        return [summed[0]] + [move(summed[d], axis, d) for d in steps]

    def spread(value, axis):
        arrived = {d: move(value, axis, d) for d in steps}
        return [value] + [arrived[d] for d in range(1, RING)]

    sum_a = first_stage(partials[:RING], "x")
    sum_b = first_stage(partials[RING:], "y")
    terms_a = second_stage(sum_a, "y")
    terms_b = second_stage(sum_b, "x")
    first = rank * 2 * half // TILE
    slope_a, pooled_a = activate(tile_table(table, first, half // TILE), terms_a)
    slope_b, pooled_b = activate(tile_table(table, first + half // TILE, half // TILE), terms_b)
    row_a, column_b = pl.pallas_call(
        collect_kernel,
        out_shape=(piece, piece),
        in_specs=[vmem] * (2 * RING),
        out_specs=(any_spec, any_spec),
        scratch_shapes=[pltpu.SemaphoreType.DMA((2 * RING,))],
        name="collect",
    )(*spread(slope_a, "x"), *spread(slope_b, "y"))
    slopes = spread(row_a, "y") + spread(column_b, "x")
    pooled = pooled_a + pooled_b

    def exchange(packed):
        mine = lax.psum_scatter(packed, "dp", scatter_dimension=0, tiled=True)
        height = packed.shape[0] // parts
        places = tile_table(table, (cap + rank * height) // TILE, height // TILE)
        slope_mine, pooled_mine = activate(places, [mine])
        return lax.all_gather(slope_mine, "dp", axis=0, tiled=True), pooled_mine

    slopes_over, pooled_over = lax.cond(
        most > cap,
        exchange,
        lambda packed: (jnp.zeros_like(packed), jnp.zeros_like(pooled)),
        over,
    )
    pooled = pooled + pooled_over

    grads_all = pl.pallas_call(
        functools.partial(hidden_grad_kernel, cap),
        out_shape=jax.ShapeDtypeStruct((batches * per_batch, plen, dslice), jnp.bfloat16),
        grid_spec=pltpu.PrefetchScalarGridSpec(
            num_scalar_prefetch=1,
            grid=(batches,),
            in_specs=[any_spec] * (2 * RING + 1) + [w_spec],
            out_specs=pl.BlockSpec((per_batch, plen, dslice), lambda i, t: (i, 0, 0)),
            scratch_shapes=[buf_shape, sems],
        ),
        compiler_params=pltpu.CompilerParams(vmem_limit_bytes=limit),
        cost_estimate=pl.CostEstimate(
            flops=flops, bytes_accessed=24 * 1024 * 1024, transcendentals=0
        ),
        name="hidden_grad",
    )(tab, *slopes, slopes_over, w_blocks)
    grad_hidden = lax.psum_scatter(grads_all, "vocab", scatter_dimension=0, tiled=True)

    pooled_parts = lax.all_to_all(
        pooled.reshape(parts, -1, BLOCK), "dp", split_axis=0, concat_axis=0, tiled=True
    )
    reps = jnp.sum(pooled_parts, axis=0).reshape(1, 1, OWN_SLOTS, col_width)

    group = 4
    moment_spec = pl.BlockSpec(
        (group, BLOCK, dslice), lambda i, t: (jnp.maximum(i - batches, 0), 0, 0)
    )
    moment_shape = jax.ShapeDtypeStruct((OWN_BLOCKS, BLOCK, dslice), jnp.bfloat16)
    new_first, new_second = pl.pallas_call(
        functools.partial(weight_grad_kernel, cap, batches),
        out_shape=(moment_shape, moment_shape),
        grid_spec=pltpu.PrefetchScalarGridSpec(
            num_scalar_prefetch=1,
            grid=(batches + OWN_BLOCKS // group,),
            in_specs=passage_specs + [any_spec] * (2 * RING + 1) + [moment_spec] * 2,
            out_specs=(moment_spec, moment_spec),
            scratch_shapes=[buf_shape, pltpu.VMEM((OWN_BLOCKS, BLOCK, dslice), jnp.float32), sems],
        ),
        compiler_params=pltpu.CompilerParams(vmem_limit_bytes=limit),
        cost_estimate=pl.CostEstimate(
            flops=flops, bytes_accessed=24 * 1024 * 1024, transcendentals=0
        ),
        name="weight_grad",
    )(
        tab,
        *([rows_all] * OWN_SLOTS),
        *slopes,
        slopes_over,
        first_moment.reshape(moment_shape.shape),
        second_moment.reshape(moment_shape.shape),
    )
    return (
        reps,
        grad_hidden,
        new_first.reshape(first_moment.shape),
        new_second.reshape(second_moment.shape),
    )


def solution(mesh):
    return jax.shard_map(
        shards,
        mesh=mesh,
        in_specs=(
            P("vocab", None, "dp"),
            P("vocab", "dp"),
            P("vocab"),
            P("vocab", "dp"),
            P("vocab", "dp"),
            P(None, "vocab", None),
            P(None, "vocab", None),
            P(),
            P(),
        ),
        out_specs=(
            P("dp", "vocab", None, None),
            P("vocab", None, "dp"),
            P("vocab", "dp"),
            P("vocab", "dp"),
        ),
        check_vma=False,
    )
```

```python
import functools

import jax
import jax.numpy as jnp
from jax import lax
from jax.experimental import pallas as pl
from jax.experimental.pallas import tpu as pltpu
from jax.sharding import PartitionSpec as P

BLOCK = 128
OWN_BLOCKS = 32
SLOT_BLOCKS = 4
OWN_SLOTS = 4
TILE = 16
RING = 4
CAP_SHARE = 15
CAP_PARTS = 32

beta_one = 0.9
beta_two = 0.999

PASS, COUNT, ROWS, OFF, LEN, IDS = 0, 1, 2, 3, 4, 5
WIDTH = 16
UNIT, START, TLEN, BIAS_ROW, COT_ROW = 0, 1, 2, 3, 4
TWIDTH = 8

CONTRACT_LAST = (((1,), (1,)), ((), ()))
CONTRACT_FIRST = (((0,), (0,)), ((), ()))


def slot_table(counts_all, ids, lengths, me):
    batches, per_batch, owners = counts_all.shape
    live = (counts_all > 0).astype(jnp.int32)
    place = jnp.arange(per_batch, dtype=jnp.int32)
    earlier = (place[None, :] < place[:, None]).astype(jnp.int32)
    rank = jnp.sum(live[:, None, :, :] * earlier[None, :, :, None], axis=2)
    slot_place = jnp.arange(OWN_SLOTS, dtype=jnp.int32)
    padded = (lengths + TILE - 1) // TILE * TILE
    kept = live * (rank < OWN_SLOTS)
    totals = jnp.sum(kept * counts_all * padded[:, :, None], axis=(0, 1))
    counts = lax.dynamic_index_in_dim(counts_all, me, 2, keepdims=False)
    live_me = lax.dynamic_index_in_dim(live, me, 2, keepdims=False)
    rank_me = lax.dynamic_index_in_dim(rank, me, 2, keepdims=False)
    chosen = (
        (live_me[:, None, :] == 1) & (rank_me[:, None, :] == slot_place[None, :, None])
    ).astype(jnp.int32)
    first = jnp.arange(batches, dtype=jnp.int32)[:, None] * per_batch
    passage = jnp.sum(chosen * place[None, None, :], axis=2) + first
    count = jnp.sum(chosen * counts[:, None, :], axis=2)
    length = jnp.sum(chosen * lengths[:, None, :], axis=2)
    rows = jnp.sum(chosen * padded[:, None, :], axis=2)
    slot_ids = jnp.sum(chosen[:, :, :, None] * ids[:, None, :, :], axis=2)
    slots = batches * OWN_SLOTS
    need = (count * rows).reshape(slots)
    order = jnp.arange(slots, dtype=jnp.int32)
    off = jnp.sum(jnp.where(order[None, :] < order[:, None], need[None, :], 0), axis=1)
    columns = [
        passage.reshape(slots, 1),
        count.reshape(slots, 1),
        rows.reshape(slots, 1),
        off.reshape(slots, 1),
        length.reshape(slots, 1),
        slot_ids.reshape(slots, SLOT_BLOCKS),
        jnp.zeros((slots, WIDTH - IDS - SLOT_BLOCKS), jnp.int32),
    ]
    return jnp.concatenate(columns, axis=1), jnp.max(totals)


def tile_table(slots, first_tile, tiles):
    at = first_tile + jnp.arange(tiles, dtype=jnp.int32)
    starts = slots[:, OFF] // TILE
    holder = jnp.sum((starts[None, :] <= at[:, None]).astype(jnp.int32), axis=1) - 1
    order = jnp.arange(slots.shape[0], dtype=jnp.int32)
    pick = (holder[:, None] == order[None, :]).astype(jnp.int32)
    mine = jnp.sum(pick[:, :, None] * slots[None, :, :], axis=1)
    height = mine[:, ROWS] // TILE
    rel = at - mine[:, OFF] // TILE
    q = sum((rel >= height * n).astype(jnp.int32) for n in range(1, SLOT_BLOCKS))
    start = (rel - q * height) * TILE
    length = jnp.where(rel < height * mine[:, COUNT], mine[:, LEN], 0)
    which = jnp.arange(SLOT_BLOCKS, dtype=jnp.int32)
    block = jnp.sum(
        jnp.where(which[None, :] == q[:, None], mine[:, IDS : IDS + SLOT_BLOCKS], 0), axis=1
    )
    columns = [
        holder * SLOT_BLOCKS + q,
        start,
        length,
        block,
        mine[:, PASS] * SLOT_BLOCKS + q,
    ]
    filler = jnp.zeros((tiles,), jnp.int32)
    return jnp.stack(columns + [filler] * (TWIDTH - len(columns)), axis=1).reshape(-1)


def slot_weights(w_ref, tab_ref, base):
    return jnp.concatenate([w_ref[tab_ref[base + IDS + q]] for q in range(SLOT_BLOCKS)], axis=0)


def slot_slopes(buf, tab_ref, base):
    plen = BLOCK
    count, rows = tab_ref[base + COUNT], tab_ref[base + ROWS]
    off, length = tab_ref[base + OFF], tab_ref[base + LEN]
    token = lax.broadcasted_iota(jnp.int32, (plen, BLOCK), 0)
    pieces = []
    for q in range(SLOT_BLOCKS):
        at = pl.multiple_of(off + q * rows, TILE)
        value = buf[pl.ds(at, plen), :]
        bound = jnp.where(q < count, length, 0)
        pieces.append(jnp.where(token < bound, value.astype(jnp.float32), 0.0).astype(jnp.bfloat16))
    return jnp.concatenate(pieces, axis=1)


def placed(tab_ref, slots, buf, pieces, sems, out):
    ahead, across = pieces[:RING], pieces[RING:]
    half = ahead[0].shape[1]
    base = slots * WIDTH
    x, y = tab_ref[base], tab_ref[base + 1]
    copies = []
    for dx in range(RING):
        for dy in range(RING):
            if out:
                to_x, to_y = x + dx, y + dy
            else:
                to_x, to_y = x - dx + RING, y - dy + RING
            owner = lax.rem(to_y, RING) * RING + lax.rem(to_x, RING)
            start = pl.multiple_of(owner * (2 * half), TILE)
            if out:
                first, second = ahead[dx].at[dy], across[dy].at[dx]
            else:
                first, second = ahead[dy].at[dx], across[dx].at[dy]
            for ref, at in ((first, start), (second, pl.multiple_of(start + half, TILE))):
                view = buf.at[pl.ds(at, half)]
                source, target = (view, ref) if out else (ref, view)
                copies.append(pltpu.make_async_copy(source, target, sems.at[len(copies)]))
    return copies


def packed_total(tab_ref, slots):
    base = (slots - 1) * WIDTH
    return tab_ref[base + OFF] + tab_ref[base + COUNT] * tab_ref[base + ROWS]


def forward_kernel(cap, tab_ref, *refs):
    hidden_refs, w_ref = refs[:OWN_SLOTS], refs[OWN_SLOTS]
    pieces = refs[OWN_SLOTS + 1 : OWN_SLOTS + 1 + 2 * RING]
    rest_ref, buf, sems = refs[OWN_SLOTS + 1 + 2 * RING :]
    j = pl.program_id(0)
    slots = pl.num_programs(0) * OWN_SLOTS
    for s in range(OWN_SLOTS):
        base = (j * OWN_SLOTS + s) * WIDTH
        rows, off = tab_ref[base + ROWS], tab_ref[base + OFF]
        value = lax.dot_general(
            hidden_refs[s][0],
            slot_weights(w_ref, tab_ref, base),
            CONTRACT_LAST,
            preferred_element_type=jnp.float32,
        ).astype(jnp.bfloat16)
        for q in range(SLOT_BLOCKS):
            at = pl.multiple_of(off + q * rows, TILE)
            buf[pl.ds(at, BLOCK), :] = value[:, q * BLOCK : (q + 1) * BLOCK]

    @pl.when(j == pl.num_programs(0) - 1)
    def _():
        copies = placed(tab_ref, slots, buf, pieces, sems, True)
        for copy in copies:
            copy.start()
        for copy in copies:
            copy.wait()

        @pl.when(packed_total(tab_ref, slots) > cap)
        def _():
            more = pltpu.make_async_copy(
                buf.at[pl.ds(cap, rest_ref.shape[0])], rest_ref, sems.at[0]
            )
            more.start()
            more.wait()


def activate_kernel(tiles, tile_ref, bias_ref, cot_ref, *refs):
    lg_refs, (slope_ref, pooled_ref) = refs[:-2], refs[-2:]
    pooled_ref[...] = jnp.zeros_like(pooled_ref)

    def step(i, carry):
        base = i * TWIDTH
        unit, start = tile_ref[base + UNIT], tile_ref[base + START]
        length, bias_row = tile_ref[base + TLEN], tile_ref[base + BIAS_ROW]
        cot_row = tile_ref[base + COT_ROW]
        at = pl.multiple_of(i * TILE, TILE)
        x = bias_ref[pl.ds(bias_row, 1), :]
        for lg_ref in lg_refs:
            x = x + lg_ref[pl.ds(at, TILE), :].astype(jnp.float32)
        token = lax.broadcasted_iota(jnp.int32, x.shape, 0) + start
        keep = token < length
        divisor = jnp.full((1, BLOCK), jnp.maximum(length, 1), jnp.int32).astype(jnp.float32)
        weight = 1.0 / divisor
        small = jnp.exp(-jnp.abs(x))
        soft = jnp.maximum(x, 0.0) + jnp.log1p(small)
        sig = jnp.where(x >= 0, 1.0, small) / (1.0 + small)
        gain = jnp.where(keep, jnp.log1p(soft) * weight, 0.0)
        pooled_ref[pl.ds(unit, 1), :] += jnp.sum(gain, axis=0, keepdims=True)
        cot = cot_ref[pl.ds(cot_row, 1), :] * weight
        slope = jnp.where(keep, cot * sig / (1.0 + soft), 0.0)
        slope_ref[pl.ds(at, TILE), :] = slope.astype(jnp.bfloat16)
        return carry

    lax.fori_loop(0, tiles, step, 0, unroll=4)


def load_slopes(cap, tab_ref, pieces, rest_ref, buf, sems, slots):
    copies = placed(tab_ref, slots, buf, pieces, sems, False)
    for copy in copies:
        copy.start()
    for copy in copies:
        copy.wait()

    @pl.when(packed_total(tab_ref, slots) > cap)
    def _():
        more = pltpu.make_async_copy(rest_ref, buf.at[pl.ds(cap, rest_ref.shape[0])], sems.at[0])
        more.start()
        more.wait()


def hidden_grad_kernel(cap, tab_ref, *refs):
    pieces = refs[: 2 * RING]
    rest_ref, w_ref, out_ref, buf, sems = refs[2 * RING :]
    j = pl.program_id(0)

    @pl.when(j == 0)
    def _():
        load_slopes(cap, tab_ref, pieces, rest_ref, buf, sems, pl.num_programs(0) * OWN_SLOTS)

    out_ref[...] = jnp.zeros_like(out_ref)
    per_batch = out_ref.shape[0]
    bases = [(j * OWN_SLOTS + s) * WIDTH for s in range(OWN_SLOTS)]
    values = [
        jnp.dot(
            slot_slopes(buf, tab_ref, base),
            slot_weights(w_ref, tab_ref, base),
            preferred_element_type=jnp.float32,
        ).astype(jnp.bfloat16)
        for base in bases
    ]
    for base, value in zip(bases, values):

        @pl.when(tab_ref[base + COUNT] > 0)
        def _():
            out_ref[tab_ref[base + PASS] - j * per_batch] = value


def weight_grad_kernel(cap, batches, tab_ref, *refs):
    hidden_refs, pieces = refs[:OWN_SLOTS], refs[OWN_SLOTS : OWN_SLOTS + 2 * RING]
    rest_ref, m_ref, v_ref, first_ref, second_ref, buf, acc, sems = refs[OWN_SLOTS + 2 * RING :]
    i = pl.program_id(0)

    @pl.when(i == 0)
    def _():
        load_slopes(cap, tab_ref, pieces, rest_ref, buf, sems, batches * OWN_SLOTS)
        acc[...] = jnp.zeros_like(acc)

    @pl.when(i < batches)
    def _():
        for s in range(OWN_SLOTS):
            base = (i * OWN_SLOTS + s) * WIDTH

            @pl.when(tab_ref[base + COUNT] > 0)
            def _():
                value = lax.dot_general(
                    slot_slopes(buf, tab_ref, base),
                    hidden_refs[s][0],
                    CONTRACT_FIRST,
                    preferred_element_type=jnp.float32,
                )
                for q in range(SLOT_BLOCKS):
                    acc[tab_ref[base + IDS + q]] += value[q * BLOCK : (q + 1) * BLOCK]

    @pl.when(i >= batches)
    def _():
        group = m_ref.shape[0]
        at = (i - batches) * group
        grad = acc[pl.ds(at, group)]
        m = m_ref[...].astype(jnp.float32)
        v = v_ref[...].astype(jnp.float32)
        first_ref[...] = (beta_one * m + (1.0 - beta_one) * grad).astype(jnp.bfloat16)
        second_ref[...] = (beta_two * v + (1.0 - beta_two) * grad * grad).astype(jnp.bfloat16)


def shards(
    hidden,
    weights,
    bias,
    first_moment,
    second_moment,
    rep_cot,
    active_blocks,
    block_counts,
    passage_len,
):
    batches = lax.axis_size("vocab")
    parts = lax.axis_size("dp")
    per_batch, plen, dslice = hidden.shape
    col_width = SLOT_BLOCKS * BLOCK
    slots = batches * OWN_SLOTS
    full = slots * SLOT_BLOCKS * plen
    cap = full * CAP_SHARE // CAP_PARTS
    rest = full - cap
    slack = 2 * BLOCK
    me = lax.axis_index("vocab")
    rank = lax.axis_index("dp")

    rows_all = lax.all_gather(hidden, "vocab", axis=0, tiled=True)

    table, most = slot_table(
        block_counts.reshape(batches, per_batch, batches),
        active_blocks.reshape(batches, per_batch, SLOT_BLOCKS),
        passage_len.reshape(batches, per_batch),
        me,
    )
    place = jnp.where(
        jnp.arange(WIDTH) == 0, lax.rem(rank, RING), jnp.where(jnp.arange(WIDTH) == 1, rank // RING, 0)
    )
    tab = jnp.concatenate([table.reshape(-1), place.astype(jnp.int32)])
    cot_rows = rep_cot.astype(jnp.float32).reshape(-1, BLOCK)
    bias_rows = bias.reshape(OWN_BLOCKS, BLOCK)
    w_blocks = weights.reshape(OWN_BLOCKS, BLOCK, dslice)

    any_spec = pl.BlockSpec(memory_space=pl.ANY)
    vmem = pl.BlockSpec(memory_space=pltpu.VMEM)
    smem = pl.BlockSpec(memory_space=pltpu.SMEM)

    def passage_spec(s):
        def index(i, t):
            row = jnp.minimum(i, batches - 1) * OWN_SLOTS + s
            return (t[row * WIDTH + PASS], 0, 0)

        return pl.BlockSpec((1, plen, dslice), index)

    passage_specs = [passage_spec(s) for s in range(OWN_SLOTS)]
    w_spec = pl.BlockSpec(
        w_blocks.shape, lambda i, t: (0, 0, 0), pipeline_mode=pl.Buffered(buffer_count=1)
    )
    buf_shape = pltpu.VMEM((full + slack, BLOCK), jnp.bfloat16)
    sems = pltpu.SemaphoreType.DMA((2 * parts,))
    half = cap // parts // 2
    piece = jax.ShapeDtypeStruct((RING, half, BLOCK), jnp.bfloat16)
    limit = 60 * 1024 * 1024
    flops = 2 * slots * plen * col_width * dslice

    *partials, over = pl.pallas_call(
        functools.partial(forward_kernel, cap),
        out_shape=(*[piece] * (2 * RING), jax.ShapeDtypeStruct((rest, BLOCK), jnp.bfloat16)),
        grid_spec=pltpu.PrefetchScalarGridSpec(
            num_scalar_prefetch=1,
            grid=(batches,),
            in_specs=passage_specs + [w_spec],
            out_specs=(any_spec,) * (2 * RING + 1),
            scratch_shapes=[buf_shape, sems],
        ),
        compiler_params=pltpu.CompilerParams(vmem_limit_bytes=limit),
        cost_estimate=pl.CostEstimate(
            flops=flops, bytes_accessed=16 * 1024 * 1024, transcendentals=0
        ),
        name="forward",
    )(tab, *([rows_all] * OWN_SLOTS), w_blocks)

    def activate(places, terms):
        height = terms[0].shape[0]
        return pl.pallas_call(
            functools.partial(activate_kernel, height // TILE),
            out_shape=(
                jax.ShapeDtypeStruct((height, BLOCK), jnp.bfloat16),
                jax.ShapeDtypeStruct((slots * SLOT_BLOCKS, BLOCK), jnp.float32),
            ),
            in_specs=[smem] + [vmem] * (2 + len(terms)),
            out_specs=(vmem, vmem),
            name="activate",
        )(places, bias_rows, cot_rows, *terms)

    def move(value, axis, step):
        pairs = []
        for y in range(RING):
            for x in range(RING):
                to_x, to_y = ((x + step) % RING, y) if axis == "x" else (x, (y + step) % RING)
                pairs.append((y * RING + x, to_y * RING + to_x))
        return lax.ppermute(value, "dp", pairs)

    steps = (1, 3, 2)

    def first_stage(terms, axis):
        arrived = [move(terms[d], axis, d) for d in steps]
        total = terms[0].astype(jnp.float32)
        for value in arrived:
            total = total + value.astype(jnp.float32)
        return total.astype(jnp.bfloat16)

    def second_stage(summed, axis):
        return [summed[0]] + [move(summed[d], axis, d) for d in steps]

    def spread(value, axis):
        arrived = {d: move(value, axis, d) for d in steps}
        return [value] + [arrived[d] for d in range(1, RING)]

    sum_a = first_stage(partials[:RING], "x")
    sum_b = first_stage(partials[RING:], "y")
    terms_a = second_stage(sum_a, "y")
    terms_b = second_stage(sum_b, "x")
    first = rank * 2 * half // TILE
    slope_a, pooled_a = activate(tile_table(table, first, half // TILE), terms_a)
    slope_b, pooled_b = activate(tile_table(table, first + half // TILE, half // TILE), terms_b)
    row_a = jnp.stack(spread(slope_a, "x"))
    column_b = jnp.stack(spread(slope_b, "y"))
    slopes = spread(row_a, "y") + spread(column_b, "x")
    pooled = pooled_a + pooled_b

    def exchange(packed):
        mine = lax.psum_scatter(packed, "dp", scatter_dimension=0, tiled=True)
        height = packed.shape[0] // parts
        places = tile_table(table, (cap + rank * height) // TILE, height // TILE)
        slope_mine, pooled_mine = activate(places, [mine])
        return lax.all_gather(slope_mine, "dp", axis=0, tiled=True), pooled_mine

    slopes_over, pooled_over = lax.cond(
        most > cap,
        exchange,
        lambda packed: (jnp.zeros_like(packed), jnp.zeros_like(pooled)),
        over,
    )
    pooled = pooled + pooled_over

    grads_all = pl.pallas_call(
        functools.partial(hidden_grad_kernel, cap),
        out_shape=jax.ShapeDtypeStruct((batches * per_batch, plen, dslice), jnp.bfloat16),
        grid_spec=pltpu.PrefetchScalarGridSpec(
            num_scalar_prefetch=1,
            grid=(batches,),
            in_specs=[any_spec] * (2 * RING + 1) + [w_spec],
            out_specs=pl.BlockSpec((per_batch, plen, dslice), lambda i, t: (i, 0, 0)),
            scratch_shapes=[buf_shape, sems],
        ),
        compiler_params=pltpu.CompilerParams(vmem_limit_bytes=limit),
        cost_estimate=pl.CostEstimate(
            flops=flops, bytes_accessed=24 * 1024 * 1024, transcendentals=0
        ),
        name="hidden_grad",
    )(tab, *slopes, slopes_over, w_blocks)
    grad_hidden = lax.psum_scatter(grads_all, "vocab", scatter_dimension=0, tiled=True)

    pooled_parts = lax.all_to_all(
        pooled.reshape(parts, -1, BLOCK), "dp", split_axis=0, concat_axis=0, tiled=True
    )
    reps = jnp.sum(pooled_parts, axis=0).reshape(1, 1, OWN_SLOTS, col_width)

    group = 4
    moment_spec = pl.BlockSpec(
        (group, BLOCK, dslice), lambda i, t: (jnp.maximum(i - batches, 0), 0, 0)
    )
    moment_shape = jax.ShapeDtypeStruct((OWN_BLOCKS, BLOCK, dslice), jnp.bfloat16)
    new_first, new_second = pl.pallas_call(
        functools.partial(weight_grad_kernel, cap, batches),
        out_shape=(moment_shape, moment_shape),
        grid_spec=pltpu.PrefetchScalarGridSpec(
            num_scalar_prefetch=1,
            grid=(batches + OWN_BLOCKS // group,),
            in_specs=passage_specs + [any_spec] * (2 * RING + 1) + [moment_spec] * 2,
            out_specs=(moment_spec, moment_spec),
            scratch_shapes=[buf_shape, pltpu.VMEM((OWN_BLOCKS, BLOCK, dslice), jnp.float32), sems],
        ),
        compiler_params=pltpu.CompilerParams(vmem_limit_bytes=limit),
        cost_estimate=pl.CostEstimate(
            flops=flops, bytes_accessed=24 * 1024 * 1024, transcendentals=0
        ),
        name="weight_grad",
    )(
        tab,
        *([rows_all] * OWN_SLOTS),
        *slopes,
        slopes_over,
        first_moment.reshape(moment_shape.shape),
        second_moment.reshape(moment_shape.shape),
    )
    return (
        reps,
        grad_hidden,
        new_first.reshape(first_moment.shape),
        new_second.reshape(second_moment.shape),
    )


def solution(mesh):
    return jax.shard_map(
        shards,
        mesh=mesh,
        in_specs=(
            P("vocab", None, "dp"),
            P("vocab", "dp"),
            P("vocab"),
            P("vocab", "dp"),
            P("vocab", "dp"),
            P(None, "vocab", None),
            P(None, "vocab", None),
            P(),
            P(),
        ),
        out_specs=(
            P("dp", "vocab", None, None),
            P("vocab", None, "dp"),
            P("vocab", "dp"),
            P("vocab", "dp"),
        ),
        check_vma=False,
    )
```
